32 devices in a mesh: slab: 8 (over z, y), row: 4 (over x, core).
Axes of the slice: x: 2, y: 2, z: 4, core: 2. Of those that a mesh axis runs over, the one named last changes fastest.
Arguments:
- queries: bfloat16 [8192, 32, 128], P('slab', 'row'), may hold values from -72 to 72, as said below
- keys: bfloat16 [8192, 32, 128], P('slab', 'row'), may hold values from -4 to 4
- values: bfloat16 [8192, 32, 128], P('slab', 'row'), may hold values from -6 to 6
- out_grad: bfloat16 [8192, 32, 128], P(('slab', 'row')), may hold values from -6 to 6
- col_start: int32 [64], replicated, may hold values from 0 to 2, as said below
- valid_tiles: int32 [8], replicated, may hold values from 4 to 8, as said below
Outputs:
- query_grad: bfloat16 [8192, 32, 128], P(('slab', 'row'))
- key_grad: bfloat16 [8192, 32, 128], P(('slab', 'row'))
- value_grad: bfloat16 [8192, 32, 128], P(('slab', 'row'))
The draws below stay inside these ranges and needn't reach their ends.
Inputs may be any that keep to these rules, and one draw needn't show every extreme that they name: `queries`: of order one in most rows. For query tile a with tile column w = (a % 8) % 4, col_start[a] is w - 1 or w, kept within 0 to 2. The tiles of a slab with index below valid_tiles hold real keys, the others padding; the values 4 and 8 occur in every draw.
All inputs are finite; a program needn't handle non-finite values.
Results may differ from the reference program's by a relative error of at most 0.0095.
Values may be sent and summed in bfloat16 or wider, within the bound.
No kernel may reach another device: no remote copies, remote signals or barrier semaphores. Data moves between devices by JAX's collectives and lax.ppermute only.
A program may use at most 256 MiB of HBM per device.

```python
import jax
import jax.numpy as jnp
from jax import lax

HEADS = 32
HD = 128
TILE = 128
GH = 2
GW = 4
WIN_COLS = 2
TPS = 8
SLABS = 8
TILES = 64
TOKENS = 8192


def keys_common(key):
    raw_keys = jnp.clip(jax.random.normal(jax.random.fold_in(key, 11), (TOKENS, HEADS, HD), jnp.float32), -3.5, 3.5)
    return raw_keys


def draw_keys(key, part):
    raw_keys = keys_common(key)
    return raw_keys.astype(jnp.bfloat16)


def draw_queries(key, part):
    drawn = jnp.clip(jax.random.normal(jax.random.fold_in(key, 13), (TOKENS, HEADS, HD), jnp.float32), -3.5, 3.5)
    return drawn.astype(jnp.bfloat16)


def draw_col_start(key, part):
    tile_ids = jnp.arange(TILES, dtype=jnp.int32)
    column = tile_ids % GW
    backward = jax.random.randint(jax.random.fold_in(key, 21), (TILES,), 0, 2, jnp.int32)
    return jnp.clip(column - backward, 0, GW - WIN_COLS).astype(jnp.int32)


def draw_valid_tiles(key, part):
    counts = jax.random.randint(jax.random.fold_in(key, 31), (SLABS,), GW, GH * GW + 1, jnp.int32)
    fuller = jax.random.randint(jax.random.fold_in(key, 32), (), 0, SLABS, jnp.int32)
    emptier = (fuller + 1 + jax.random.randint(jax.random.fold_in(key, 33), (), 0, SLABS - 1, jnp.int32)) % SLABS
    slab_ids = jnp.arange(SLABS, dtype=jnp.int32)
    counts = jnp.where(slab_ids == fuller, GH * GW, counts)
    counts = jnp.where(slab_ids == emptier, GW, counts)
    return counts.astype(jnp.int32)


def levels(key, shape, split, low, largest):
    def one(dim, blocks):
        draws = jax.random.uniform(jax.random.fold_in(jax.random.fold_in(key, 6), dim), (blocks,), jnp.float32, low / len(split), largest / len(split))
        return jnp.repeat(jnp.exp(draws), shape[dim] // blocks).reshape((-1,) + (1,) * (len(shape) - dim - 1))

    level = one(*split[0])
    for cut in split[1:]:
        level = level * one(*cut)
    return level


def scatter_about(stream_key, shape, deviation, bound, shards=(), kind=jnp.bfloat16):
    level = levels(stream_key, shape, shards, -0.22, 0.18) if shards else 1.0
    result = jax.random.normal(stream_key, shape, jnp.float32) * deviation * level
    return jnp.minimum(jnp.maximum(result, -bound), bound).astype(kind)


def setup_inputs(seed: int = 0) -> dict:
    key_of = jax.random.split(jax.random.key(seed), 7)
    queries = draw_queries(jax.random.fold_in(key_of[6], 71), 0)
    keys = draw_keys(jax.random.fold_in(key_of[6], 71), 0)
    values = scatter_about(key_of[2], (TOKENS, HEADS, HD), 1.0, 6.0, ((0, 8), (1, 4)))
    out_grad = scatter_about(key_of[3], (TOKENS, HEADS, HD), 1.0, 6.0, ((0, 32),))
    col_start = draw_col_start(jax.random.fold_in(key_of[6], 71), 0)
    valid_tiles = draw_valid_tiles(jax.random.fold_in(key_of[6], 71), 0)
    return dict(queries=queries, keys=keys, values=values, out_grad=out_grad, col_start=col_start, valid_tiles=valid_tiles)


def window_tiles(col_first, slab_pos, valid_tiles):
    per_row = GH * WIN_COLS
    slot_ids = jnp.arange(3 * per_row, dtype=jnp.int32)
    slab_step = slot_ids // per_row
    inner_slot = slot_ids % per_row
    tile_base = slab_step * TPS + (inner_slot // WIN_COLS) * GW + inner_slot % WIN_COLS
    key_tiles = tile_base[None, :] + col_first[:, None]
    key_slab = slab_pos - 1 + slab_step
    slab_ids = jnp.arange(SLABS, dtype=jnp.int32)
    counts = jnp.sum(jnp.where(slab_ids[None, :] == key_slab[:, None], valid_tiles[None, :], 0), axis=1)
    key_valid = (key_slab[None, :] >= 0) & (key_slab[None, :] < SLABS) & (key_tiles - slab_step[None, :] * TPS < counts[None, :])
    return key_tiles, key_valid


def reference(queries, keys, values, out_grad, col_start, valid_tiles):
    tok_slab = TPS * TILE
    inv_root = HD ** -0.5
    padding = jnp.zeros((tok_slab, HEADS, HD), keys.dtype)
    keys_padded = jnp.concatenate([padding, keys, padding], axis=0)
    values_padded = jnp.concatenate([padding, values, padding], axis=0)

    def slab_body(running, slab_pos):
        key_sums, value_sums = running
        row_start = slab_pos * tok_slab
        query_block = lax.dynamic_slice_in_dim(queries, row_start, tok_slab, 0).astype(jnp.float32).reshape(TPS, TILE, HEADS, HD)
        grad_rows = lax.dynamic_slice_in_dim(out_grad, row_start, tok_slab, 0).astype(jnp.float32).reshape(TPS, TILE, HEADS, HD)
        key_ext = lax.dynamic_slice_in_dim(keys_padded, row_start, 3 * tok_slab, 0).astype(jnp.float32).reshape(3 * TPS, TILE, HEADS, HD)
        value_ext = lax.dynamic_slice_in_dim(values_padded, row_start, 3 * tok_slab, 0).astype(jnp.float32).reshape(3 * TPS, TILE, HEADS, HD)
        col_first = lax.dynamic_slice_in_dim(col_start, slab_pos * TPS, TPS, 0)
        key_tiles, key_valid = window_tiles(col_first, slab_pos, valid_tiles)
        slot_count = key_tiles.shape[1]
        key_sel = key_ext[key_tiles].reshape(TPS, slot_count * TILE, HEADS, HD)
        value_sel = value_ext[key_tiles].reshape(TPS, slot_count * TILE, HEADS, HD)
        valid_wide = jnp.repeat(key_valid, TILE, axis=1)[:, None, None, :]
        scores = jnp.einsum('nqhd,nkhd->nhqk', query_block, key_sel) * inv_root
        scores = jnp.where(valid_wide, scores, -jnp.inf)
        row_max = jnp.max(scores, axis=-1, keepdims=True)
        expo_vals = jnp.exp(scores - row_max)
        attend = expo_vals / jnp.sum(expo_vals, axis=-1, keepdims=True)
        attend_b = lax.optimization_barrier(attend.astype(jnp.bfloat16)).astype(jnp.float32)
        output = jnp.einsum('nhqk,nkhd->nqhd', attend_b, value_sel)
        row_delta = jnp.einsum('nqhd,nqhd->nhq', grad_rows, output)
        grad_attend = jnp.einsum('nqhd,nkhd->nhqk', grad_rows, value_sel)
        grad_scores = lax.optimization_barrier((attend * (grad_attend - row_delta[..., None])).astype(jnp.bfloat16)).astype(jnp.float32)
        query_grad = jnp.einsum('nhqk,nkhd->nqhd', grad_scores, key_sel) * inv_root
        key_grad = jnp.einsum('nhqk,nqhd->nkhd', grad_scores, query_block) * inv_root
        value_grad = jnp.einsum('nhqk,nqhd->nkhd', attend_b, grad_rows)
        tile_shape = (TPS, slot_count, TILE, HEADS, HD)
        key_part = jnp.zeros((3 * TPS, TILE, HEADS, HD), jnp.float32).at[key_tiles].add(key_grad.reshape(tile_shape))
        value_part = jnp.zeros((3 * TPS, TILE, HEADS, HD), jnp.float32).at[key_tiles].add(value_grad.reshape(tile_shape))
        key_sums = lax.dynamic_update_slice_in_dim(key_sums, lax.dynamic_slice_in_dim(key_sums, row_start, 3 * tok_slab, 0) + key_part.reshape(3 * tok_slab, HEADS, HD), row_start, 0)
        value_sums = lax.dynamic_update_slice_in_dim(value_sums, lax.dynamic_slice_in_dim(value_sums, row_start, 3 * tok_slab, 0) + value_part.reshape(3 * tok_slab, HEADS, HD), row_start, 0)
        return (key_sums, value_sums), query_grad.reshape(tok_slab, HEADS, HD)

    zero_sums = jnp.zeros(((SLABS + 2) * tok_slab, HEADS, HD), jnp.float32)
    (key_sums, value_sums), query_rows = lax.scan(slab_body, (zero_sums, zero_sums), jnp.arange(SLABS, dtype=jnp.int32))
    query_grad = query_rows.reshape(TOKENS, HEADS, HD).astype(jnp.bfloat16)
    key_grad = key_sums[tok_slab:tok_slab + TOKENS].astype(jnp.bfloat16)
    value_grad = value_sums[tok_slab:tok_slab + TOKENS].astype(jnp.bfloat16)
    return query_grad, key_grad, value_grad
```

```python
import functools
import math

import jax
import jax.numpy as jnp
from jax import lax
from jax.experimental import pallas as pl
from jax.experimental.pallas import tpu as pltpu
from jax.sharding import PartitionSpec as P

TILE = 128
GH = 2
GW = 4
WIN_COLS = 2
TPS = GH * GW
SPAN = WIN_COLS * TILE
NEG = -1e30


def attention_kernel(row_count, scalars, *refs):
    q_keep, q_recv = refs[:2]
    do_refs = refs[2 : 2 + row_count]
    kv_low, kv_keep, kv_recv, kv_high = refs[2 + row_count : 6 + row_count]
    outs = refs[6 + row_count : 12 + row_count]
    dq_keep, dq_recv, own_keep, own_recv, half_low, half_high = outs
    q_buf, do_buf, k_buf, v_buf, kt_buf, dk_acc, dv_acc, p_buf, dp_buf = refs[12 + row_count :]
    tok = q_keep.shape[0]
    head_dim = q_keep.shape[1]
    scale = head_dim ** (-0.5)
    part = tok // row_count

    q_buf[pl.ds(0, tok), :] = q_keep[...]
    q_buf[pl.ds(tok, tok), :] = q_recv[...]
    for step, do_ref in enumerate(do_refs):
        start = scalars[2 * TPS + 4 + step] * part
        for side in range(2):
            where = pl.multiple_of(side * tok + start, part)
            do_buf[pl.ds(where, part), :] = do_ref[side]
    for slot, ref in enumerate((kv_low, kv_keep, kv_recv, kv_high)):
        k_buf[pl.ds(slot * tok, tok), :] = ref[0]
        v_buf[pl.ds(slot * tok, tok), :] = ref[1]
        kt_buf[:, pl.ds(slot * tok, tok)] = ref[0].T
    dk_acc[...] = jnp.zeros_like(dk_acc)
    dv_acc[...] = jnp.zeros_like(dv_acc)

    def unit(side, col, q_starts):
        width = TILE * len(q_starts)

        def rows_of(buf):
            parts = [buf[pl.ds(start, TILE), :] for start in q_starts]
            return parts[0] if len(parts) == 1 else jnp.concatenate(parts, axis=0)

        q = rows_of(q_buf)
        do = rows_of(do_buf)
        blocks = 3 * GH
        offsets = []
        limits = []
        for block in range(blocks):
            step, grid_row = block // GH, block % GH
            offset = (side + step) * tok + grid_row * GW * TILE + col * TILE
            offsets.append(pl.multiple_of(offset, TILE))
            count = scalars[2 * TPS + side + step]
            limits.append((count - grid_row * GW - col) * TILE)
        key_row = lax.broadcasted_iota(jnp.int32, (SPAN, width), 0)
        top = jnp.full((8, width), NEG, jnp.float32)
        for block in range(blocks):
            scores = lax.dot_general(
                k_buf[pl.ds(offsets[block], SPAN), :],
                q,
                (((1,), (1,)), ((), ())),
                preferred_element_type=jnp.float32,
            )
            scores = jnp.where(key_row < limits[block], scores, NEG)
            p_buf[pl.ds(block * SPAN, SPAN), pl.ds(0, width)] = scores
            top = jnp.maximum(top, jnp.max(scores.reshape(SPAN // 8, 8, width), axis=0))
        top = jnp.max(top, axis=0, keepdims=True)
        total = jnp.zeros((8, width), jnp.float32)
        delta = jnp.zeros((8, width), jnp.float32)
        for block in range(blocks):
            here = pl.ds(block * SPAN, SPAN), pl.ds(0, width)
            expo = jnp.exp2((p_buf[here] - top) * (scale * math.log2(math.e)))
            grad = lax.dot_general(
                v_buf[pl.ds(offsets[block], SPAN), :],
                do,
                (((1,), (1,)), ((), ())),
                preferred_element_type=jnp.float32,
            )
            p_buf[here] = expo
            dp_buf[here] = grad
            total += jnp.sum(expo.reshape(SPAN // 8, 8, width), axis=0)
            delta += jnp.sum((expo * grad).reshape(SPAN // 8, 8, width), axis=0)
        inverse = 1.0 / jnp.sum(total, axis=0, keepdims=True)
        delta = jnp.sum(delta, axis=0, keepdims=True) * inverse
        dq_t = jnp.zeros((head_dim, width), jnp.float32)
        for block in range(blocks):
            here = pl.ds(block * SPAN, SPAN), pl.ds(0, width)
            keys_here = pl.ds(offsets[block], SPAN)
            attend = p_buf[here] * inverse
            grad_scores = (attend * (dp_buf[here] - delta)).astype(jnp.bfloat16)
            attend_b = attend.astype(jnp.bfloat16)
            dv_acc[keys_here, :] += jnp.dot(attend_b, do, preferred_element_type=jnp.float32)
            dk_acc[keys_here, :] += jnp.dot(grad_scores, q, preferred_element_type=jnp.float32)
            dq_t += jnp.dot(kt_buf[:, keys_here], grad_scores, preferred_element_type=jnp.float32)
        dq = (dq_t * scale).T.astype(jnp.bfloat16)
        for place, start in enumerate(q_starts):
            q_buf[pl.ds(start, TILE), :] = dq[place * TILE : (place + 1) * TILE]

    def step(index, carry):
        side = index // GW
        column = index % GW
        first = scalars[side * TPS + column]
        second = scalars[side * TPS + GW + column]
        start0 = pl.multiple_of(side * tok + column * TILE, TILE)
        start1 = pl.multiple_of(side * tok + (GW + column) * TILE, TILE)

        @pl.when(first == second)
        def _():
            unit(side, first, [start0, start1])

        @pl.when(first != second)
        def _():
            def single(which, inner):
                start = pl.multiple_of(start0 + which * (GW * TILE), TILE)
                unit(side, jnp.where(which == 0, first, second), [start])
                return inner

            lax.fori_loop(0, GH, single, 0)

        return carry

    lax.fori_loop(0, 2 * GW, step, 0)
    dq_keep[...] = q_buf[pl.ds(0, tok), :]
    dq_recv[...] = q_buf[pl.ds(tok, tok), :]
    for place, (acc, factor) in enumerate(((dk_acc, scale), (dv_acc, None))):
        for slot, ref in enumerate((half_low, own_keep, own_recv, half_high)):
            part_sum = acc[pl.ds(slot * tok, tok), :]
            if factor is not None:
                part_sum = part_sum * factor
            ref[place] = part_sum.astype(ref.dtype)


def attention_call(scalars, q_keep, q_recv, do_parts, kv_low, kv_keep, kv_recv, kv_high):
    tok, head_dim = q_keep.shape
    row_count = len(do_parts)
    vmem = pl.BlockSpec(memory_space=pltpu.VMEM)
    keys_all = 4 * tok
    window = 3 * GH * SPAN
    pairs = 2 * TPS * TILE * window
    return pl.pallas_call(
        functools.partial(attention_kernel, row_count),
        out_shape=(
            jax.ShapeDtypeStruct((tok, head_dim), jnp.bfloat16),
            jax.ShapeDtypeStruct((tok, head_dim), jnp.bfloat16),
            jax.ShapeDtypeStruct((2, tok, head_dim), jnp.float32),
            jax.ShapeDtypeStruct((2, tok, head_dim), jnp.float32),
            jax.ShapeDtypeStruct((2, tok, head_dim), jnp.bfloat16),
            jax.ShapeDtypeStruct((2, tok, head_dim), jnp.bfloat16),
        ),
        in_specs=[pl.BlockSpec(memory_space=pltpu.SMEM)] + [vmem] * (6 + row_count),
        out_specs=(vmem,) * 6,
        scratch_shapes=[
            pltpu.VMEM((2 * tok, head_dim), jnp.bfloat16),
            pltpu.VMEM((2 * tok, head_dim), jnp.bfloat16),
            pltpu.VMEM((keys_all, head_dim), jnp.bfloat16),
            pltpu.VMEM((keys_all, head_dim), jnp.bfloat16),
            pltpu.VMEM((head_dim, keys_all), jnp.bfloat16),
            pltpu.VMEM((keys_all, head_dim), jnp.float32),
            pltpu.VMEM((keys_all, head_dim), jnp.float32),
            pltpu.VMEM((window, GH * TILE), jnp.float32),
            pltpu.VMEM((window, GH * TILE), jnp.float32),
        ],
        cost_estimate=pl.CostEstimate(
            flops=10 * pairs * head_dim, transcendentals=pairs, bytes_accessed=16 * tok * head_dim * 2
        ),
        compiler_params=pltpu.CompilerParams(vmem_limit_bytes=40 * 2**20),
        name="window_grads",
    )(scalars, q_keep, q_recv, *do_parts, kv_low, kv_keep, kv_recv, kv_high)


def assemble_kernel(row_count, head_count, scalars, *refs):
    pieces, (out_ref, held) = refs[:-2], refs[-2:]
    chunks = len(pieces) // (2 * row_count)
    index = 0
    for chunk in range(chunks):
        for group in range(2):
            for step in range(row_count):
                source = scalars[step]
                side = scalars[row_count + group]
                head = source * (2 * chunks) + side * chunks + chunk
                held[head] = pieces[index][0]
                index += 1
    out_ref[...] = jnp.swapaxes(held[...], 0, 1)


def on_device(mesh_shape, queries, keys, values, out_grad, col_start, valid_tiles):
    tok, heads_here, head_dim = queries.shape
    row_count = mesh_shape["row"]
    slab_total = mesh_shape["slab"]
    keep_count = heads_here // 2
    part = tok // row_count
    slab_pos = lax.axis_index("slab")
    row_pos = lax.axis_index("row")
    parity = slab_pos % 2
    partner = slab_pos + 1 - 2 * parity

    swap = [(s, s ^ 1) for s in range(slab_total)]
    out_high = [(s, s - 2 if s % 2 == 0 else s + 2) for s in range(slab_total)]
    out_high = [(s, t) for s, t in out_high if 0 <= t < slab_total]
    out_low = [(s, s + 2 if s % 2 == 0 else s - 2) for s in range(slab_total)]
    out_low = [(s, t) for s, t in out_low if 0 <= t < slab_total]

    def move(array, axis, pairs):
        return lax.ppermute(array, axis, pairs)

    def turned(pairs):
        return [(t, s) for s, t in pairs]

    def row_exchange(array, dim):
        got = []
        for step in range(row_count):
            target = row_pos ^ step
            piece = lax.dynamic_slice_in_dim(array, target * part, part, axis=dim)
            if step:
                piece = move(piece, "row", [(r, r ^ step) for r in range(row_count)])
            got.append(piece)
        return got

    slab_ids = jnp.stack(
        [
            jnp.where(parity == 0, slab_pos - 1, slab_pos + 1),
            slab_pos,
            partner,
            jnp.where(parity == 0, slab_pos + 2, slab_pos - 2),
        ]
    )
    inside = (slab_ids >= 0) & (slab_ids < slab_total)
    counts = jnp.where(inside, valid_tiles[jnp.clip(slab_ids, 0, slab_total - 1)], 0)
    row_ids = row_pos ^ jnp.arange(row_count, dtype=jnp.int32)
    scalars = jnp.concatenate(
        [
            lax.dynamic_slice_in_dim(col_start, slab_pos * TPS, TPS, 0),
            lax.dynamic_slice_in_dim(col_start, partner * TPS, TPS, 0),
            counts.astype(jnp.int32),
            row_ids,
        ]
    )

    def head_major(array):
        turned_array = jnp.swapaxes(array, 0, 1)
        return turned_array.reshape((-1, 2, keep_count) + turned_array.shape[1:])

    def pick(array, side, chunk):
        return lax.dynamic_index_in_dim(array[:, :, chunk], side, axis=1, keepdims=False)

    k_major, v_major = head_major(keys), head_major(values)
    q_major, do_major = head_major(queries), head_major(out_grad)

    inputs = []
    for chunk in range(keep_count):
        kv_sent = jnp.concatenate(
            [pick(k_major, 1 - parity, chunk), pick(v_major, 1 - parity, chunk)]
        )
        kv_keep = jnp.concatenate([pick(k_major, parity, chunk), pick(v_major, parity, chunk)])
        kv_recv = move(kv_sent, "slab", swap)
        kv_high = move(kv_keep, "slab", out_high)
        kv_low = move(kv_recv, "slab", out_low)
        do_keep = pick(do_major, parity, chunk)
        do_recv = move(pick(do_major, 1 - parity, chunk), "slab", swap)
        q_keep = pick(q_major, parity, chunk)[0]
        q_recv = move(pick(q_major, 1 - parity, chunk)[0], "slab", swap)
        both = jnp.stack([do_keep, do_recv], axis=1)
        do_parts = []
        for step in range(row_count):
            piece = lax.dynamic_index_in_dim(both, row_pos ^ step, axis=0, keepdims=False)
            if step:
                piece = move(piece, "row", [(r, r ^ step) for r in range(row_count)])
            do_parts.append(piece)
        inputs.append((q_keep, q_recv, do_parts, kv_low, kv_keep, kv_recv, kv_high))

    pieces = [[[] for _ in range(keep_count)] for _ in range(3)]
    for chunk in range(keep_count):
        dq_keep, dq_recv, own_keep, own_recv, half_low, half_high = attention_call(
            scalars, *inputs[chunk]
        )
        dq_back = move(dq_recv, "slab", swap)
        add_keep = move(half_high, "slab", turned(out_high))
        add_recv = move(half_low, "slab", turned(out_low))
        kv_grad = (own_keep + add_keep.astype(jnp.float32)).astype(jnp.bfloat16)
        kv_sent = (own_recv + add_recv.astype(jnp.float32)).astype(jnp.bfloat16)
        kv_back = move(kv_sent, "slab", swap)
        dq_parts = row_exchange(jnp.stack([dq_keep, dq_back]), 1)
        keep_parts = row_exchange(kv_grad, 1)
        back_parts = row_exchange(kv_back, 1)
        pieces[0][chunk] = [[x[0] for x in dq_parts], [x[1] for x in dq_parts]]
        pieces[1][chunk] = [[x[0] for x in keep_parts], [x[0] for x in back_parts]]
        pieces[2][chunk] = [[x[1] for x in keep_parts], [x[1] for x in back_parts]]

    def assembled(per_chunk):
        stacked = jnp.stack(
            [
                jnp.stack([jnp.stack(per_chunk[chunk][group]) for chunk in range(keep_count)], 1)
                for group in range(2)
            ],
            1,
        )
        stacked = stacked[row_ids]
        stacked = jnp.where(parity == 0, stacked, stacked[:, ::-1])
        stacked = stacked.reshape(row_count * heads_here, part, head_dim)
        return jnp.swapaxes(stacked, 0, 1)

    return tuple(assembled(per_chunk) for per_chunk in pieces)


def solution(mesh):
    placed = (
        P("slab", "row", None),
        P("slab", "row", None),
        P("slab", "row", None),
        P(("slab", "row"), None, None),
        P(),
        P(),
    )
    return jax.shard_map(
        functools.partial(on_device, dict(mesh.shape)),
        mesh=mesh,
        in_specs=placed,
        out_specs=(P(("slab", "row"), None, None),) * 3,
        check_vma=False,
    )
```

```python
import math

import jax
import jax.numpy as jnp
from jax import lax
from jax.experimental import pallas as pl
from jax.experimental.pallas import tpu as pltpu
from jax.sharding import PartitionSpec as P


TILE = 128
GH = 2
GW = 4
WIN_COLS = 2
TPS = GH * GW
SPAN = WIN_COLS * TILE
NEG = -1e30


def attention_kernel(
    scalars,
    q_keep,
    q_recv,
    do_ref,
    kv_low,
    kv_keep,
    kv_recv,
    kv_high,
    dq_keep,
    dq_recv,
    own_keep,
    own_recv,
    half_low,
    half_high,
    q_buf,
    do_buf,
    k_buf,
    v_buf,
    kt_buf,
    dk_acc,
    dv_acc,
    p_buf,
    dp_buf,
):
    tok, head_dim = q_keep.shape
    scale = head_dim ** (-0.5)
    parity = scalars[2 * TPS + 4]

    q_buf[pl.ds(0, tok), :] = q_keep[...]
    q_buf[pl.ds(tok, tok), :] = q_recv[...]
    senders, _, part, _ = do_ref.shape
    for sender in range(senders):
        do_buf[pl.ds(sender * part, part), :] = do_ref[sender, 0]
    for slot, ref in enumerate((kv_low, kv_keep, kv_recv, kv_high)):
        k_buf[pl.ds(slot * tok, tok), :] = ref[0]
        v_buf[pl.ds(slot * tok, tok), :] = ref[1]
        kt_buf[:, pl.ds(slot * tok, tok)] = ref[0].T
    dk_acc[...] = jnp.zeros_like(dk_acc)
    dv_acc[...] = jnp.zeros_like(dv_acc)

    def unit(side, col, q_starts):
        width = TILE * len(q_starts)
        turn = ((side + parity) % 2 - side) * tok

        def rows_of(buf, shift):
            parts = [
                buf[pl.ds(pl.multiple_of(start + shift, TILE), TILE), :] for start in q_starts
            ]
            return parts[0] if len(parts) == 1 else jnp.concatenate(parts, axis=0)

        q = rows_of(q_buf, 0)
        do = rows_of(do_buf, turn)
        blocks = 3 * GH
        offsets = []
        limits = []
        for block in range(blocks):
            step, grid_row = block // GH, block % GH
            offset = (side + step) * tok + grid_row * GW * TILE + col * TILE
            offsets.append(pl.multiple_of(offset, TILE))
            count = scalars[2 * TPS + side + step]
            limits.append((count - grid_row * GW - col) * TILE)
        key_row = lax.broadcasted_iota(jnp.int32, (SPAN, width), 0)
        top = jnp.full((8, width), NEG, jnp.float32)
        for block in range(blocks):
            scores = lax.dot_general(
                k_buf[pl.ds(offsets[block], SPAN), :],
                q,
                (((1,), (1,)), ((), ())),
                preferred_element_type=jnp.float32,
            )
            scores = jnp.where(key_row < limits[block], scores, NEG)
            p_buf[pl.ds(block * SPAN, SPAN), pl.ds(0, width)] = scores
            top = jnp.maximum(top, jnp.max(scores.reshape(SPAN // 8, 8, width), axis=0))
        top = jnp.max(top, axis=0, keepdims=True)
        total = jnp.zeros((8, width), jnp.float32)
        delta = jnp.zeros((8, width), jnp.float32)
        for block in range(blocks):
            here = pl.ds(block * SPAN, SPAN), pl.ds(0, width)
            expo = jnp.exp2((p_buf[here] - top) * (scale * math.log2(math.e)))
            grad = lax.dot_general(
                v_buf[pl.ds(offsets[block], SPAN), :],
                do,
                (((1,), (1,)), ((), ())),
                preferred_element_type=jnp.float32,
            )
            p_buf[here] = expo
            dp_buf[here] = grad
            total += jnp.sum(expo.reshape(SPAN // 8, 8, width), axis=0)
            delta += jnp.sum((expo * grad).reshape(SPAN // 8, 8, width), axis=0)
        inverse = 1.0 / jnp.sum(total, axis=0, keepdims=True)
        delta = jnp.sum(delta, axis=0, keepdims=True) * inverse
        dq_t = jnp.zeros((head_dim, width), jnp.float32)
        for block in range(blocks):
            here = pl.ds(block * SPAN, SPAN), pl.ds(0, width)
            keys_here = pl.ds(offsets[block], SPAN)
            attend = p_buf[here] * inverse
            grad_scores = (attend * (dp_buf[here] - delta)).astype(jnp.bfloat16)
            attend_b = attend.astype(jnp.bfloat16)
            dv_acc[keys_here, :] += jnp.dot(attend_b, do, preferred_element_type=jnp.float32)
            dk_acc[keys_here, :] += jnp.dot(grad_scores, q, preferred_element_type=jnp.float32)
            dq_t += jnp.dot(kt_buf[:, keys_here], grad_scores, preferred_element_type=jnp.float32)
        dq = (dq_t * scale).T.astype(jnp.bfloat16)
        for place, start in enumerate(q_starts):
            q_buf[pl.ds(start, TILE), :] = dq[place * TILE : (place + 1) * TILE]

    def step(index, carry):
        side = index // GW
        column = index % GW
        first = scalars[side * TPS + column]
        second = scalars[side * TPS + GW + column]
        start0 = pl.multiple_of(side * tok + column * TILE, TILE)
        start1 = pl.multiple_of(side * tok + (GW + column) * TILE, TILE)

        @pl.when(first == second)
        def _():
            unit(side, first, [start0, start1])

        @pl.when(first != second)
        def _():
            def single(which, inner):
                start = pl.multiple_of(start0 + which * (GW * TILE), TILE)
                unit(side, jnp.where(which == 0, first, second), [start])
                return inner

            lax.fori_loop(0, GH, single, 0)

        return carry

    lax.fori_loop(0, 2 * GW, step, 0)
    dq_keep[...] = q_buf[pl.ds(0, tok), :]
    dq_recv[...] = q_buf[pl.ds(tok, tok), :]
    for place, (acc, factor) in enumerate(((dk_acc, scale), (dv_acc, None))):
        for slot, ref in enumerate((half_low, own_keep, own_recv, half_high)):
            part_sum = acc[pl.ds(slot * tok, tok), :]
            if factor is not None:
                part_sum = part_sum * factor
            ref[place] = part_sum.astype(ref.dtype)


def attention_call(scalars, chunk, q_keep, q_recv, do_all, kv_low, kv_keep, kv_recv, kv_high):
    tok, head_dim = q_keep.shape
    senders, _, part, _ = do_all.shape
    whole = pl.BlockSpec((tok, head_dim), lambda i: (0, 0))
    pair = pl.BlockSpec((2, tok, head_dim), lambda i: (0, 0, 0))
    do_spec = pl.BlockSpec((senders, 1, part, head_dim), lambda i: (0, chunk, 0, 0))
    keys_all = 4 * tok
    window = 3 * GH * SPAN
    pairs = 2 * TPS * TILE * window
    return pl.pallas_call(
        attention_kernel,
        grid=(1,),
        out_shape=(jax.ShapeDtypeStruct((tok, head_dim), jnp.bfloat16),) * 2
        + (jax.ShapeDtypeStruct((2, tok, head_dim), jnp.float32),) * 2
        + (jax.ShapeDtypeStruct((2, tok, head_dim), jnp.bfloat16),) * 2,
        in_specs=[pl.BlockSpec(memory_space=pltpu.SMEM), whole, whole, do_spec] + [pair] * 4,
        out_specs=(whole,) * 2 + (pair,) * 4,
        scratch_shapes=[
            pltpu.VMEM((2 * tok, head_dim), jnp.bfloat16),
            pltpu.VMEM((2 * tok, head_dim), jnp.bfloat16),
            pltpu.VMEM((keys_all, head_dim), jnp.bfloat16),
            pltpu.VMEM((keys_all, head_dim), jnp.bfloat16),
            pltpu.VMEM((head_dim, keys_all), jnp.bfloat16),
            pltpu.VMEM((keys_all, head_dim), jnp.float32),
            pltpu.VMEM((keys_all, head_dim), jnp.float32),
            pltpu.VMEM((window, GH * TILE), jnp.float32),
            pltpu.VMEM((window, GH * TILE), jnp.float32),
        ],
        cost_estimate=pl.CostEstimate(
            flops=10 * pairs * head_dim, transcendentals=pairs, bytes_accessed=16 * tok * head_dim * 2
        ),
        name="window_grads",
    )(scalars, q_keep, q_recv, do_all, kv_low, kv_keep, kv_recv, kv_high)


def split_kernel(scalars, *refs):
    (first, second), outs, held = refs[:2], refs[2:-1], refs[-1]
    chunks = len(outs) // 2
    side = scalars[0]
    for place, ref in enumerate((first, second)):
        held[...] = jnp.swapaxes(ref[...], 0, 1)
        for chunk in range(chunks):
            outs[chunk][place] = held[(1 - side) * chunks + chunk]
            outs[chunks + chunk][place] = held[side * chunks + chunk]


def split_pair(scalars, first, second):
    tok, heads_here, head_dim = first.shape
    steps = TPS
    block = tok // steps
    chunks = heads_here // 2
    spec = pl.BlockSpec((block, heads_here, head_dim), lambda i: (i, 0, 0))
    out_spec = pl.BlockSpec((2, block, head_dim), lambda i: (0, i, 0))
    outs = pl.pallas_call(
        split_kernel,
        grid=(steps,),
        out_shape=(jax.ShapeDtypeStruct((2, tok, head_dim), first.dtype),) * (2 * chunks),
        in_specs=[pl.BlockSpec(memory_space=pltpu.SMEM), spec, spec],
        out_specs=(out_spec,) * (2 * chunks),
        scratch_shapes=[pltpu.VMEM((heads_here, block, head_dim), first.dtype)],
        name="split_pair",
    )(scalars, first, second)
    return outs[:chunks], outs[chunks:]


def spread_kernel(scalars, queries, out_grad, *refs):
    outs, do_out, held_q, held_do = refs[:-3], refs[-3], refs[-2], refs[-1]
    side = scalars[0]
    heads_here = held_q.shape[0]
    chunks = heads_here // 2
    row_count = held_do.shape[0] // heads_here
    held_q[...] = jnp.swapaxes(queries[...], 0, 1)
    for chunk in range(chunks):
        outs[chunk][...] = held_q[(1 - side) * chunks + chunk]
        outs[chunks + chunk][...] = held_q[side * chunks + chunk]
    held_do[...] = jnp.swapaxes(out_grad[...], 0, 1)
    for group in range(2):
        for row in range(row_count):
            head = row * heads_here + group * chunks
            do_out[group * row_count + row] = held_do[head : head + chunks]


def spread(scalars, queries, out_grad):
    tok, heads_here, head_dim = queries.shape
    part, heads, _ = out_grad.shape
    steps = min(TPS, part // 16)
    chunks = heads_here // 2
    targets = 2 * heads // heads_here
    outs = pl.pallas_call(
        spread_kernel,
        grid=(steps,),
        out_shape=(jax.ShapeDtypeStruct((tok, head_dim), queries.dtype),) * (2 * chunks)
        + (jax.ShapeDtypeStruct((targets, chunks, part, head_dim), queries.dtype),),
        in_specs=[
            pl.BlockSpec(memory_space=pltpu.SMEM),
            pl.BlockSpec((tok // steps, heads_here, head_dim), lambda i: (i, 0, 0)),
            pl.BlockSpec((part // steps, heads, head_dim), lambda i: (i, 0, 0)),
        ],
        out_specs=(pl.BlockSpec((tok // steps, head_dim), lambda i: (i, 0)),) * (2 * chunks)
        + (pl.BlockSpec((targets, chunks, part // steps, head_dim), lambda i: (0, 0, i, 0)),),
        scratch_shapes=[
            pltpu.VMEM((heads_here, tok // steps, head_dim), queries.dtype),
            pltpu.VMEM((heads, part // steps, head_dim), queries.dtype),
        ],
        name="spread",
    )(scalars, queries, out_grad)
    return outs[:chunks], outs[chunks : 2 * chunks], outs[-1]


def merge_kernel(scalars, dq_keep, dq_recv, own_keep, own_recv, add_keep, add_recv, out):
    targets, _, part, _ = out.shape
    row_count = targets // 2
    side = scalars[0]
    groups = ((dq_keep, own_keep, add_keep, side), (dq_recv, own_recv, add_recv, 1 - side))
    for grad, own, add, place in groups:
        for row in range(row_count):
            rows = pl.ds(row * part, part)
            target = place * row_count + row
            out[target, 0] = grad[rows, :]
            for which in range(2):
                total = own[which, rows, :] + add[which, rows, :].astype(jnp.float32)
                out[target, 1 + which] = total.astype(out.dtype)


def merge(scalars, row_count, dq_keep, dq_recv, own_keep, own_recv, add_keep, add_recv):
    tok, head_dim = dq_keep.shape
    vmem = pl.BlockSpec(memory_space=pltpu.VMEM)
    return pl.pallas_call(
        merge_kernel,
        out_shape=jax.ShapeDtypeStruct((2 * row_count, 3, tok // row_count, head_dim), jnp.bfloat16),
        in_specs=[pl.BlockSpec(memory_space=pltpu.SMEM)] + [vmem] * 6,
        out_specs=vmem,
        name="merge",
    )(scalars, dq_keep, dq_recv, own_keep, own_recv, add_keep, add_recv)


def assemble_kernel(*refs):
    chunks = len(refs) - 4
    pieces, outs, held = refs[:chunks], refs[chunks:-1], refs[-1]
    senders = pieces[0].shape[0]
    for plane in range(3):
        for chunk in range(chunks):
            for group in range(2):
                for row in range(senders // 2):
                    head = row * 2 * chunks + group * chunks + chunk
                    held[head] = pieces[chunk][group * (senders // 2) + row, plane]
        outs[plane][...] = jnp.swapaxes(held[...], 0, 1)


def assemble(pieces):
    chunks = len(pieces)
    senders, _, part, head_dim = pieces[0].shape
    heads = chunks * senders
    steps = min(TPS, part // 16)
    block = part // steps
    return pl.pallas_call(
        assemble_kernel,
        grid=(steps,),
        out_shape=(jax.ShapeDtypeStruct((part, heads, head_dim), jnp.bfloat16),) * 3,
        in_specs=[pl.BlockSpec((senders, 3, block, head_dim), lambda i: (0, 0, i, 0))] * chunks,
        out_specs=(pl.BlockSpec((block, heads, head_dim), lambda i: (i, 0, 0)),) * 3,
        scratch_shapes=[pltpu.VMEM((heads, block, head_dim), jnp.bfloat16)],
        name="assemble",
    )(*pieces)


def on_device(mesh_shape, queries, keys, values, out_grad, col_start, valid_tiles):
    _, heads_here, _ = queries.shape
    row_count = mesh_shape["row"]
    slab_total = mesh_shape["slab"]
    chunks = heads_here // 2
    slab_pos = lax.axis_index("slab")
    parity = slab_pos % 2
    partner = slab_pos + 1 - 2 * parity

    swap = [(s, s ^ 1) for s in range(slab_total)]
    out_high = [(s, s - 2 if s % 2 == 0 else s + 2) for s in range(slab_total)]
    out_high = [(s, t) for s, t in out_high if 0 <= t < slab_total]
    out_low = [(s, s + 2 if s % 2 == 0 else s - 2) for s in range(slab_total)]
    out_low = [(s, t) for s, t in out_low if 0 <= t < slab_total]

    def turned(pairs):
        return [(t, s) for s, t in pairs]

    def over_slab(array, pairs):
        return lax.ppermute(array, "slab", pairs)

    groups = [
        list(range(first, first + 2 * row_count))
        for first in range(0, slab_total * row_count, 2 * row_count)
    ]

    def to_all(array):
        return lax.all_to_all(
            array, ("slab", "row"), 0, 0, axis_index_groups=groups, tiled=True
        )

    slab_ids = jnp.stack(
        [
            jnp.where(parity == 0, slab_pos - 1, slab_pos + 1),
            slab_pos,
            partner,
            jnp.where(parity == 0, slab_pos + 2, slab_pos - 2),
        ]
    )
    inside = (slab_ids >= 0) & (slab_ids < slab_total)
    counts = jnp.where(inside, valid_tiles[jnp.clip(slab_ids, 0, slab_total - 1)], 0)
    places = parity.reshape(1)
    scalars = jnp.concatenate(
        [
            lax.dynamic_slice_in_dim(col_start, slab_pos * TPS, TPS, 0),
            lax.dynamic_slice_in_dim(col_start, partner * TPS, TPS, 0),
            counts.astype(jnp.int32),
            places,
        ]
    )

    kv_sent, kv_keep = split_pair(places, keys, values)
    q_sent, q_keep, do_sent = spread(places, queries, out_grad)
    do_all = to_all(do_sent)
    inputs = []
    for chunk in range(chunks):
        kv_recv = over_slab(kv_sent[chunk], swap)
        kv_high = over_slab(kv_keep[chunk], out_high)
        kv_low = over_slab(kv_recv, out_low)
        q_recv = over_slab(q_sent[chunk], swap)
        inputs.append((q_keep[chunk], q_recv, do_all, kv_low, kv_keep[chunk], kv_recv, kv_high))

    pieces = []
    for chunk in range(chunks):
        dq_keep, dq_recv, own_keep, own_recv, half_low, half_high = attention_call(
            scalars, chunk, *inputs[chunk]
        )
        add_keep = over_slab(half_high, turned(out_high))
        add_recv = over_slab(half_low, turned(out_low))
        merged = merge(places, row_count, dq_keep, dq_recv, own_keep, own_recv, add_keep, add_recv)
        pieces.append(to_all(merged))
    return tuple(assemble(pieces))


def solution(mesh):
    placed = (
        P("slab", "row", None),
        P("slab", "row", None),
        P("slab", "row", None),
        P(("slab", "row"), None, None),
        P(),
        P(),
    )

    def body(*operands):
        return on_device(dict(mesh.shape), *operands)

    return jax.shard_map(
        body,
        mesh=mesh,
        in_specs=placed,
        out_specs=(P(("slab", "row"), None, None),) * 3,
        check_vma=False,
    )
```

```python
import functools
import math

import jax
import jax.numpy as jnp
from jax import lax
from jax.experimental import pallas as pl
from jax.experimental.pallas import tpu as pltpu
from jax.sharding import PartitionSpec as P


TILE = 128
GH = 2
GW = 4
WIN_COLS = 2
TPS = GH * GW
SPAN = WIN_COLS * TILE
NEG = -1e30


def attention_kernel(
    place_in_group,
    scalars,
    q_keep,
    q_recv,
    do_ref,
    kv_low,
    kv_keep,
    kv_recv,
    kv_high,
    dq_keep,
    dq_recv,
    own_keep,
    own_recv,
    half_low,
    half_high,
    q_buf,
    do_buf,
    k_buf,
    v_buf,
    low_buf,
    high_buf,
    dk_acc,
    dv_acc,
    p_buf,
    dp_buf,
    sems,
):
    tok, head_dim = q_keep.shape
    scale = head_dim ** (-0.5)
    parity = scalars[2 * TPS + 4]
    senders, _, part, _ = do_ref.shape
    count = 0

    def begin(source, target):
        nonlocal count
        copy = pltpu.make_async_copy(source, target, sems.at[count])
        count += 1
        copy.start()
        return copy

    loads = []
    for slot, ref in enumerate((kv_low, kv_keep, kv_recv, kv_high)):
        rows = pl.ds(slot * tok, tok)
        if slot == 1:
            loads += [begin(q_keep, q_buf.at[pl.ds(0, tok), :])]
            for sender in range(senders):
                rows_do = pl.ds(sender * part, part)
                loads += [begin(do_ref.at[sender, place_in_group], do_buf.at[rows_do, :])]
        late = [begin(ref.at[0], k_buf.at[rows, :]), begin(ref.at[1], v_buf.at[rows, :])]
        loads += late if slot < 3 else []
    late += [begin(q_recv, q_buf.at[pl.ds(tok, tok), :])]
    dk_acc[...] = jnp.zeros_like(dk_acc)
    dv_acc[...] = jnp.zeros_like(dv_acc)
    for copy in loads:
        copy.wait()

    def unit(side, col, q_starts):
        width = TILE * len(q_starts)
        turn = ((side + parity) % 2 - side) * tok

        def rows_of(buf, shift):
            parts = [
                buf[pl.ds(pl.multiple_of(start + shift, TILE), TILE), :] for start in q_starts
            ]
            return parts[0] if len(parts) == 1 else jnp.concatenate(parts, axis=0)

        q = rows_of(q_buf, 0)
        do = rows_of(do_buf, turn)
        blocks = 3 * GH
        offsets = []
        limits = []
        for block in range(blocks):
            step, grid_row = block // GH, block % GH
            offset = (side + step) * tok + grid_row * GW * TILE + col * TILE
            offsets.append(pl.multiple_of(offset, TILE))
            count = scalars[2 * TPS + side + step]
            limits.append((count - grid_row * GW - col) * TILE)
        key_row = lax.broadcasted_iota(jnp.int32, (SPAN, width), 0)
        top = jnp.full((8, width), NEG, jnp.float32)
        for block in range(blocks):
            scores = lax.dot_general(
                k_buf[pl.ds(offsets[block], SPAN), :],
                q,
                (((1,), (1,)), ((), ())),
                preferred_element_type=jnp.float32,
            )
            if block != GH:
                scores = jnp.where(key_row < limits[block], scores, NEG)
            p_buf[pl.ds(block * SPAN, SPAN), pl.ds(0, width)] = scores
            top = jnp.maximum(top, jnp.max(scores.reshape(SPAN // 8, 8, width), axis=0))
        top = jnp.max(top, axis=0, keepdims=True)
        total = jnp.zeros((8, width), jnp.float32)
        delta = jnp.zeros((8, width), jnp.float32)
        for block in range(blocks):
            here = pl.ds(block * SPAN, SPAN), pl.ds(0, width)
            expo = jnp.exp2((p_buf[here] - top) * (scale * math.log2(math.e)))
            grad = lax.dot_general(
                v_buf[pl.ds(offsets[block], SPAN), :],
                do,
                (((1,), (1,)), ((), ())),
                preferred_element_type=jnp.float32,
            )
            p_buf[here] = expo
            dp_buf[here] = grad
            total += jnp.sum(expo.reshape(SPAN // 8, 8, width), axis=0)
            delta += jnp.sum((expo * grad).reshape(SPAN // 8, 8, width), axis=0)
        inverse = 1.0 / jnp.sum(total, axis=0, keepdims=True)
        delta = jnp.sum(delta, axis=0, keepdims=True) * inverse
        dq = jnp.zeros((width, head_dim), jnp.float32)
        for block in range(blocks):
            here = pl.ds(block * SPAN, SPAN), pl.ds(0, width)
            keys_here = pl.ds(offsets[block], SPAN)
            attend = p_buf[here] * inverse
            grad_scores = (attend * (dp_buf[here] - delta)).astype(jnp.bfloat16)
            attend_b = attend.astype(jnp.bfloat16)
            dv_acc[keys_here, :] += jnp.dot(attend_b, do, preferred_element_type=jnp.float32)
            dk_acc[keys_here, :] += jnp.dot(grad_scores, q, preferred_element_type=jnp.float32)
            dq += lax.dot_general(
                grad_scores,
                k_buf[keys_here, :],
                (((0,), (0,)), ((), ())),
                preferred_element_type=jnp.float32,
            )
        dq = (dq * scale).astype(jnp.bfloat16)
        for place, start in enumerate(q_starts):
            q_buf[pl.ds(start, TILE), :] = dq[place * TILE : (place + 1) * TILE]

    def step(index, carry):
        side = index // GW
        column = index % GW
        first = scalars[side * TPS + column]
        second = scalars[side * TPS + GW + column]
        start0 = pl.multiple_of(side * tok + column * TILE, TILE)
        start1 = pl.multiple_of(side * tok + (GW + column) * TILE, TILE)

        @pl.when(first == second)
        def _():
            unit(side, first, [start0, start1])

        @pl.when(first != second)
        def _():
            def single(which, inner):
                start = pl.multiple_of(start0 + which * (GW * TILE), TILE)
                unit(side, jnp.where(which == 0, first, second), [start])
                return inner

            lax.fori_loop(0, GH, single, 0)

        return carry

    lax.fori_loop(0, GW, step, 0)
    for copy in late:
        copy.wait()
    stores = [begin(q_buf.at[pl.ds(0, tok), :], dq_keep)]
    low_buf[0] = (dk_acc[pl.ds(0, tok), :] * scale).astype(low_buf.dtype)
    low_buf[1] = dv_acc[pl.ds(0, tok), :].astype(low_buf.dtype)
    stores += [begin(low_buf, half_low)]
    lax.fori_loop(GW, 2 * GW, step, 0)
    stores += [begin(q_buf.at[pl.ds(tok, tok), :], dq_recv)]
    for slot, ref in ((1, own_keep), (2, own_recv)):
        rows = pl.ds(slot * tok, tok)
        stores += [begin(dk_acc.at[rows, :], ref.at[0]), begin(dv_acc.at[rows, :], ref.at[1])]
    high_buf[0] = (dk_acc[pl.ds(3 * tok, tok), :] * scale).astype(high_buf.dtype)
    high_buf[1] = dv_acc[pl.ds(3 * tok, tok), :].astype(high_buf.dtype)
    stores += [begin(high_buf, half_high)]
    for copy in stores:
        copy.wait()


def attention_call(scalars, place_in_group, q_keep, q_recv, do_all, kv_low, kv_keep, kv_recv, kv_high):
    tok, head_dim = q_keep.shape
    senders, _, _, _ = do_all.shape
    place = pl.BlockSpec(memory_space=pl.ANY)
    keys_all = 4 * tok
    window = 3 * GH * SPAN
    pairs = 2 * TPS * TILE * window
    return pl.pallas_call(
        functools.partial(attention_kernel, place_in_group),
        out_shape=(jax.ShapeDtypeStruct((tok, head_dim), jnp.bfloat16),) * 2
        + (jax.ShapeDtypeStruct((2, tok, head_dim), jnp.float32),) * 2
        + (jax.ShapeDtypeStruct((2, tok, head_dim), jnp.bfloat16),) * 2,
        in_specs=[pl.BlockSpec(memory_space=pltpu.SMEM)] + [place] * 7,
        out_specs=(place,) * 6,
        scratch_shapes=[
            pltpu.VMEM((2 * tok, head_dim), jnp.bfloat16),
            pltpu.VMEM((2 * tok, head_dim), jnp.bfloat16),
            pltpu.VMEM((keys_all, head_dim), jnp.bfloat16),
            pltpu.VMEM((keys_all, head_dim), jnp.bfloat16),
            pltpu.VMEM((2, tok, head_dim), jnp.bfloat16),
            pltpu.VMEM((2, tok, head_dim), jnp.bfloat16),
            pltpu.VMEM((keys_all, head_dim), jnp.float32),
            pltpu.VMEM((keys_all, head_dim), jnp.float32),
            pltpu.VMEM((window, GH * TILE), jnp.float32),
            pltpu.VMEM((window, GH * TILE), jnp.float32),
            pltpu.SemaphoreType.DMA((18 + senders,)),
        ],
        cost_estimate=pl.CostEstimate(
            flops=10 * pairs * head_dim, transcendentals=pairs, bytes_accessed=16 * tok * head_dim * 2
        ),
        name="window_grads",
    )(scalars, q_keep, q_recv, do_all, kv_low, kv_keep, kv_recv, kv_high)


def split_kernel(scalars, *refs):
    (first, second), outs, held = refs[:2], refs[2:-1], refs[-1]
    chunks = len(outs) // 2
    side = scalars[0]
    for place, ref in enumerate((first, second)):
        held[...] = jnp.swapaxes(ref[...], 0, 1)
        for chunk in range(chunks):
            outs[chunk][place] = held[(1 - side) * chunks + chunk]
            outs[chunks + chunk][place] = held[side * chunks + chunk]


def split_pair(scalars, first, second):
    tok, heads_here, head_dim = first.shape
    steps = TPS // 2
    block = tok // steps
    chunks = heads_here // 2
    spec = pl.BlockSpec((block, heads_here, head_dim), lambda i: (i, 0, 0))
    out_spec = pl.BlockSpec((2, block, head_dim), lambda i: (0, i, 0))
    outs = pl.pallas_call(
        split_kernel,
        grid=(steps,),
        out_shape=(jax.ShapeDtypeStruct((2, tok, head_dim), first.dtype),) * (2 * chunks),
        in_specs=[pl.BlockSpec(memory_space=pltpu.SMEM), spec, spec],
        out_specs=(out_spec,) * (2 * chunks),
        scratch_shapes=[pltpu.VMEM((heads_here, block, head_dim), first.dtype)],
        name="split_pair",
    )(scalars, first, second)
    return outs[:chunks], outs[chunks:]


def chunk_groups(chunks):
    first = max(1, chunks // 2)
    return [range(first)] + ([range(first, chunks)] if first < chunks else [])


def spread_kernel(scalars, queries, out_grad, *refs):
    outs, held_q, held_do = refs[:-2], refs[-2], refs[-1]
    side = scalars[0]
    heads_here = held_q.shape[0]
    chunks = heads_here // 2
    row_count = held_do.shape[0] // heads_here
    held_q[...] = jnp.swapaxes(queries[...], 0, 1)
    for chunk in range(chunks):
        outs[chunk][...] = held_q[(1 - side) * chunks + chunk]
        outs[chunks + chunk][...] = held_q[side * chunks + chunk]
    held_do[...] = jnp.swapaxes(out_grad[...], 0, 1)
    for out, members in zip(outs[2 * chunks :], chunk_groups(chunks)):
        for group in range(2):
            for row in range(row_count):
                head = row * heads_here + group * chunks + members[0]
                out[group * row_count + row] = held_do[head : head + len(members)]


def spread(scalars, queries, out_grad):
    tok, heads_here, head_dim = queries.shape
    part, heads, _ = out_grad.shape
    steps = min(TPS // 2, part // 16)
    chunks = heads_here // 2
    targets = 2 * heads // heads_here
    sizes = [len(members) for members in chunk_groups(chunks)]
    outs = pl.pallas_call(
        spread_kernel,
        grid=(steps,),
        out_shape=(jax.ShapeDtypeStruct((tok, head_dim), queries.dtype),) * (2 * chunks)
        + tuple(
            jax.ShapeDtypeStruct((targets, size, part, head_dim), queries.dtype) for size in sizes
        ),
        in_specs=[
            pl.BlockSpec(memory_space=pltpu.SMEM),
            pl.BlockSpec((tok // steps, heads_here, head_dim), lambda i: (i, 0, 0)),
            pl.BlockSpec((part // steps, heads, head_dim), lambda i: (i, 0, 0)),
        ],
        out_specs=(pl.BlockSpec((tok // steps, head_dim), lambda i: (i, 0)),) * (2 * chunks)
        + tuple(
            pl.BlockSpec((targets, size, part // steps, head_dim), lambda i: (0, 0, i, 0))
            for size in sizes
        ),
        scratch_shapes=[
            pltpu.VMEM((heads_here, tok // steps, head_dim), queries.dtype),
            pltpu.VMEM((heads, part // steps, head_dim), queries.dtype),
        ],
        name="spread",
    )(scalars, queries, out_grad)
    return outs[:chunks], outs[chunks : 2 * chunks], outs[2 * chunks :]


def merge_kernel(scalars, own_keep, own_recv, add_keep, add_recv, *refs):
    query_grads, out = refs[:-1], refs[-1]
    targets, _, part, head_dim = out.shape
    row_count = targets // 2
    side = scalars[0]
    factors = (head_dim ** (-0.5), 1.0)
    sums = ((own_keep, add_keep, side), (own_recv, add_recv, 1 - side))
    for which, (own, add, place) in enumerate(sums):
        for row in range(row_count):
            rows = pl.ds(row * part, part)
            target = place * row_count + row
            for plane, factor in enumerate(factors):
                total = own[plane, rows, :] * factor + add[plane, rows, :].astype(jnp.float32)
                out[target, plane] = total.astype(out.dtype)
            for plane, grad in enumerate(query_grads[which::2]):
                out[target, 2 + plane] = grad[rows, :]


def merge(scalars, row_count, own_keep, own_recv, add_keep, add_recv, query_grads):
    _, tok, head_dim = own_keep.shape
    vmem = pl.BlockSpec(memory_space=pltpu.VMEM)
    flat = [grad for pair in query_grads for grad in pair]
    shape = (2 * row_count, 2 + len(query_grads), tok // row_count, head_dim)
    return pl.pallas_call(
        merge_kernel,
        out_shape=jax.ShapeDtypeStruct(shape, jnp.bfloat16),
        in_specs=[pl.BlockSpec(memory_space=pltpu.SMEM)] + [vmem] * (4 + len(flat)),
        out_specs=vmem,
        name="merge",
    )(scalars, own_keep, own_recv, add_keep, add_recv, *flat)


def query_place(chunk):
    return (0, 2) if chunk == 0 else (chunk - 1, 3 if chunk == 1 else 2)


def assemble_kernel(*refs):
    chunks = len(refs) - 4
    pieces, outs, held = refs[:chunks], refs[chunks:-1], refs[-1]
    row_count = pieces[0].shape[0] // 2
    for index, out in enumerate(outs):
        for chunk in range(chunks):
            message, plane = query_place(chunk) if index == 0 else (chunk, index - 1)
            for group in range(2):
                for row in range(row_count):
                    head = row * 2 * chunks + group * chunks + chunk
                    held[head] = pieces[message][group * row_count + row, plane]
        out[...] = jnp.swapaxes(held[...], 0, 1)


def assemble(pieces):
    chunks = len(pieces)
    senders, _, part, head_dim = pieces[0].shape
    heads = chunks * senders
    steps = min(TPS // 2, part // 16)
    block = part // steps
    return pl.pallas_call(
        assemble_kernel,
        grid=(steps,),
        out_shape=(jax.ShapeDtypeStruct((part, heads, head_dim), jnp.bfloat16),) * 3,
        in_specs=[
            pl.BlockSpec((senders, piece.shape[1], block, head_dim), lambda i: (0, 0, i, 0))
            for piece in pieces
        ],
        out_specs=(pl.BlockSpec((block, heads, head_dim), lambda i: (i, 0, 0)),) * 3,
        scratch_shapes=[pltpu.VMEM((heads, block, head_dim), jnp.bfloat16)],
        name="assemble",
    )(*pieces)


def on_device(mesh_shape, queries, keys, values, out_grad, col_start, valid_tiles):
    _, heads_here, _ = queries.shape
    row_count = mesh_shape["row"]
    slab_total = mesh_shape["slab"]
    chunks = heads_here // 2
    slab_pos = lax.axis_index("slab")
    parity = slab_pos % 2
    partner = slab_pos + 1 - 2 * parity

    swap = [(s, s ^ 1) for s in range(slab_total)]
    out_high = [(s, s - 2 if s % 2 == 0 else s + 2) for s in range(slab_total)]
    out_high = [(s, t) for s, t in out_high if 0 <= t < slab_total]
    out_low = [(s, s + 2 if s % 2 == 0 else s - 2) for s in range(slab_total)]
    out_low = [(s, t) for s, t in out_low if 0 <= t < slab_total]

    def turned(pairs):
        return [(t, s) for s, t in pairs]

    def over_slab(array, pairs):
        return lax.ppermute(array, "slab", pairs)

    groups = [
        list(range(first, first + 2 * row_count))
        for first in range(0, slab_total * row_count, 2 * row_count)
    ]

    def to_all(array):
        return lax.all_to_all(
            array, ("slab", "row"), 0, 0, axis_index_groups=groups, tiled=True
        )

    slab_ids = jnp.stack(
        [
            jnp.where(parity == 0, slab_pos - 1, slab_pos + 1),
            slab_pos,
            partner,
            jnp.where(parity == 0, slab_pos + 2, slab_pos - 2),
        ]
    )
    inside = (slab_ids >= 0) & (slab_ids < slab_total)
    counts = jnp.where(inside, valid_tiles[jnp.clip(slab_ids, 0, slab_total - 1)], 0)
    places = parity.reshape(1)
    scalars = jnp.concatenate(
        [
            lax.dynamic_slice_in_dim(col_start, slab_pos * TPS, TPS, 0),
            lax.dynamic_slice_in_dim(col_start, partner * TPS, TPS, 0),
            counts.astype(jnp.int32),
            places,
        ]
    )

    kv_sent, kv_keep = split_pair(places, keys, values)
    q_sent, q_keep, do_sent = spread(places, queries, out_grad)
    do_of = {}
    for index, members in enumerate(chunk_groups(chunks)):
        arrived = to_all(do_sent[index])
        for place, chunk in enumerate(members):
            do_of[chunk] = (place, arrived)
    inputs = []
    for chunk in range(chunks):
        kv_recv = over_slab(kv_sent[chunk], swap)
        kv_high = over_slab(kv_keep[chunk], out_high)
        kv_low = over_slab(kv_recv, out_low)
        q_recv = over_slab(q_sent[chunk], swap)
        place, do_all = do_of[chunk]
        inputs.append(
            (place, q_keep[chunk], q_recv, do_all, kv_low, kv_keep[chunk], kv_recv, kv_high)
        )

    query_grads = []
    partial_sums = []
    for chunk in range(chunks):
        dq_keep, dq_recv, own_keep, own_recv, half_low, half_high = attention_call(
            scalars, *inputs[chunk]
        )
        add_keep = over_slab(half_high, turned(out_high))
        add_recv = over_slab(half_low, turned(out_low))
        query_grads.append((dq_keep, dq_recv))
        partial_sums.append((own_keep, own_recv, add_keep, add_recv))
    pieces = []
    for chunk in range(chunks):
        own = [query_grads[other] for other in range(chunks) if query_place(other)[0] == chunk]
        merged = merge(places, row_count, *partial_sums[chunk], own)
        pieces.append(to_all(merged))
    return tuple(assemble(pieces))


def solution(mesh):
    placed = (
        P("slab", "row", None),
        P("slab", "row", None),
        P("slab", "row", None),
        P(("slab", "row"), None, None),
        P(),
        P(),
    )

    def body(*operands):
        return on_device(dict(mesh.shape), *operands)

    return jax.shard_map(
        body,
        mesh=mesh,
        in_specs=placed,
        out_specs=(P(("slab", "row"), None, None),) * 3,
        check_vma=False,
    )
```

```python
import functools
import math

import jax
import jax.numpy as jnp
from jax import lax
from jax.experimental import pallas as pl
from jax.experimental.pallas import tpu as pltpu
from jax.sharding import PartitionSpec as P


TILE = 128
GH = 2
GW = 4
WIN_COLS = 2
TPS = GH * GW
SPAN = WIN_COLS * TILE
NEG = -1e30

ALL_VMEM = pltpu.CompilerParams(vmem_limit_bytes=67_043_328)


def chunk_groups(chunks):
    first = max(1, chunks // 2)
    return [range(first)] + ([range(first, chunks)] if first < chunks else [])


def lead_groups(chunks):
    return [range(1)] + ([range(1, chunks)] if chunks > 1 else [])


def query_groups(chunks):
    bounds = [0, 1, 2, chunks]
    return [range(a, min(b, chunks)) for a, b in zip(bounds, bounds[1:]) if a < min(b, chunks)]


def group_of(groups, chunk):
    return next(index for index, members in enumerate(groups) if chunk in members)


def place_of(groups, chunk):
    return groups[group_of(groups, chunk)].index(chunk)


def attention_kernel(
    chunk,
    scalars,
    q_keep,
    q_recv,
    do_ref,
    kv_low,
    kv_keep,
    kv_recv,
    kv_high,
    dq_keep,
    dq_recv,
    own_keep,
    own_recv,
    half_low,
    half_high,
    q_buf,
    do_buf,
    k_buf,
    v_buf,
    low_buf,
    high_buf,
    dk_acc,
    dv_acc,
    p_buf,
    dp_buf,
    sems,
):
    _, tok, head_dim = q_keep.shape
    chunks = q_keep.shape[0]
    scale = head_dim ** (-0.5)
    parity = scalars[2 * TPS + 4]
    senders, _, part, _ = do_ref.shape
    do_place = place_of(chunk_groups(chunks), chunk)
    place = place_of(lead_groups(chunks), chunk)
    kv_keep, kv_high = kv_keep.at[place], kv_high.at[place]
    q_recv = q_recv.at[place_of(query_groups(chunks), chunk)]
    q_keep = q_keep.at[chunk]
    count = 0

    def begin(source, target):
        nonlocal count
        copy = pltpu.make_async_copy(source, target, sems.at[count])
        count += 1
        copy.start()
        return copy

    loads = []
    for slot, ref in enumerate((kv_low, kv_keep, kv_recv, kv_high)):
        rows = pl.ds(slot * tok, tok)
        if slot == 1:
            loads += [begin(q_keep, q_buf.at[pl.ds(0, tok), :])]
            for sender in range(senders):
                rows_do = pl.ds(sender * part, part)
                loads += [begin(do_ref.at[sender, do_place], do_buf.at[rows_do, :])]
        late = [begin(ref.at[0], k_buf.at[rows, :]), begin(ref.at[1], v_buf.at[rows, :])]
        loads += late if slot < 3 else []
    late += [begin(q_recv, q_buf.at[pl.ds(tok, tok), :])]
    dk_acc[...] = jnp.zeros_like(dk_acc)
    dv_acc[...] = jnp.zeros_like(dv_acc)
    for copy in loads:
        copy.wait()

    def unit(side, col, q_starts):
        width = TILE * len(q_starts)
        turn = ((side + parity) % 2 - side) * tok

        def rows_of(buf, shift):
            parts = [
                buf[pl.ds(pl.multiple_of(start + shift, TILE), TILE), :] for start in q_starts
            ]
            return parts[0] if len(parts) == 1 else jnp.concatenate(parts, axis=0)

        q = rows_of(q_buf, 0)
        do = rows_of(do_buf, turn)
        blocks = 3 * GH
        offsets = []
        limits = []
        for block in range(blocks):
            step, grid_row = block // GH, block % GH
            offset = (side + step) * tok + grid_row * GW * TILE + col * TILE
            offsets.append(pl.multiple_of(offset, TILE))
            count = scalars[2 * TPS + side + step]
            limits.append((count - grid_row * GW - col) * TILE)
        key_row = lax.broadcasted_iota(jnp.int32, (SPAN, width), 0)
        top = jnp.full((8, width), NEG, jnp.float32)
        for block in range(blocks):
            scores = lax.dot_general(
                k_buf[pl.ds(offsets[block], SPAN), :],
                q,
                (((1,), (1,)), ((), ())),
                preferred_element_type=jnp.float32,
            )
            if block != GH:
                scores = jnp.where(key_row < limits[block], scores, NEG)
            p_buf[pl.ds(block * SPAN, SPAN), pl.ds(0, width)] = scores
            top = jnp.maximum(top, jnp.max(scores.reshape(SPAN // 8, 8, width), axis=0))
        top = jnp.max(top, axis=0, keepdims=True)
        total = jnp.zeros((8, width), jnp.float32)
        delta = jnp.zeros((8, width), jnp.float32)
        for block in range(blocks):
            here = pl.ds(block * SPAN, SPAN), pl.ds(0, width)
            expo = jnp.exp2((p_buf[here] - top) * (scale * math.log2(math.e)))
            grad = lax.dot_general(
                v_buf[pl.ds(offsets[block], SPAN), :],
                do,
                (((1,), (1,)), ((), ())),
                preferred_element_type=jnp.float32,
            )
            p_buf[here] = expo
            dp_buf[here] = grad
            total += jnp.sum(expo.reshape(SPAN // 8, 8, width), axis=0)
            delta += jnp.sum((expo * grad).reshape(SPAN // 8, 8, width), axis=0)
        inverse = 1.0 / jnp.sum(total, axis=0, keepdims=True)
        delta = jnp.sum(delta, axis=0, keepdims=True) * inverse
        dq = jnp.zeros((width, head_dim), jnp.float32)
        for block in range(blocks):
            here = pl.ds(block * SPAN, SPAN), pl.ds(0, width)
            keys_here = pl.ds(offsets[block], SPAN)
            attend = p_buf[here] * inverse
            grad_scores = (attend * (dp_buf[here] - delta)).astype(jnp.bfloat16)
            attend_b = attend.astype(jnp.bfloat16)
            dv_acc[keys_here, :] += jnp.dot(attend_b, do, preferred_element_type=jnp.float32)
            dk_acc[keys_here, :] += jnp.dot(grad_scores, q, preferred_element_type=jnp.float32)
            dq += lax.dot_general(
                grad_scores,
                k_buf[keys_here, :],
                (((0,), (0,)), ((), ())),
                preferred_element_type=jnp.float32,
            )
        dq = (dq * scale).astype(jnp.bfloat16)
        for place, start in enumerate(q_starts):
            q_buf[pl.ds(start, TILE), :] = dq[place * TILE : (place + 1) * TILE]

    def run_side(side):
        def tile_at(index):
            column, which = index // GH, index % GH
            first = scalars[side * TPS + column]
            second = scalars[side * TPS + GW + column]
            row = jnp.where(first <= second, which, GH - 1 - which)
            start = side * tok + (row * GW + column) * TILE
            return jnp.where(row == 0, first, second), pl.multiple_of(start, TILE)

        def step(index):
            col, start = tile_at(index)
            next_col, next_start = tile_at(jnp.minimum(index + 1, TPS - 1))
            double = (index + 1 < TPS) & (col == next_col)

            @pl.when(double)
            def _():
                unit(side, col, [start, next_start])

            @pl.when(jnp.logical_not(double))
            def _():
                unit(side, col, [start])

            return index + 1 + double.astype(jnp.int32)

        lax.while_loop(lambda index: index < TPS, step, jnp.int32(0))

    run_side(0)
    for copy in late:
        copy.wait()
    stores = [begin(q_buf.at[pl.ds(0, tok), :], dq_keep)]
    low_buf[0] = (dk_acc[pl.ds(0, tok), :] * scale).astype(low_buf.dtype)
    low_buf[1] = dv_acc[pl.ds(0, tok), :].astype(low_buf.dtype)
    stores += [begin(low_buf, half_low)]
    run_side(1)
    stores += [begin(q_buf.at[pl.ds(tok, tok), :], dq_recv)]
    for slot, ref in ((1, own_keep), (2, own_recv)):
        rows = pl.ds(slot * tok, tok)
        stores += [begin(dk_acc.at[rows, :], ref.at[0]), begin(dv_acc.at[rows, :], ref.at[1])]
    high_buf[0] = (dk_acc[pl.ds(3 * tok, tok), :] * scale).astype(high_buf.dtype)
    high_buf[1] = dv_acc[pl.ds(3 * tok, tok), :].astype(high_buf.dtype)
    stores += [begin(high_buf, half_high)]
    for copy in stores:
        copy.wait()


def attention_call(scalars, chunk, q_keep, q_recv, do_all, kv_low, kv_keep, kv_recv, kv_high):
    _, tok, head_dim = q_keep.shape
    senders = do_all.shape[0]
    place = pl.BlockSpec(memory_space=pl.ANY)
    keys_all = 4 * tok
    window = 3 * GH * SPAN
    pairs = 2 * TPS * TILE * window
    return pl.pallas_call(
        functools.partial(attention_kernel, chunk),
        out_shape=(jax.ShapeDtypeStruct((tok, head_dim), jnp.bfloat16),) * 2
        + (jax.ShapeDtypeStruct((2, tok, head_dim), jnp.float32),) * 2
        + (jax.ShapeDtypeStruct((2, tok, head_dim), jnp.bfloat16),) * 2,
        in_specs=[pl.BlockSpec(memory_space=pltpu.SMEM)] + [place] * 7,
        out_specs=(place,) * 6,
        scratch_shapes=[
            pltpu.VMEM((2 * tok, head_dim), jnp.bfloat16),
            pltpu.VMEM((2 * tok, head_dim), jnp.bfloat16),
            pltpu.VMEM((keys_all, head_dim), jnp.bfloat16),
            pltpu.VMEM((keys_all, head_dim), jnp.bfloat16),
            pltpu.VMEM((2, tok, head_dim), jnp.bfloat16),
            pltpu.VMEM((2, tok, head_dim), jnp.bfloat16),
            pltpu.VMEM((keys_all, head_dim), jnp.float32),
            pltpu.VMEM((keys_all, head_dim), jnp.float32),
            pltpu.VMEM((window, GH * TILE), jnp.float32),
            pltpu.VMEM((window, GH * TILE), jnp.float32),
            pltpu.SemaphoreType.DMA((18 + senders,)),
        ],
        cost_estimate=pl.CostEstimate(
            flops=10 * pairs * head_dim, transcendentals=pairs, bytes_accessed=16 * tok * head_dim * 2
        ),
        compiler_params=ALL_VMEM,
        name="window_grads",
    )(scalars, q_keep, q_recv, do_all, kv_low, kv_keep, kv_recv, kv_high)


def split_kernel(scalars, *refs):
    (first, second), outs, held = refs[:2], refs[2:-1], refs[-1]
    chunks = held.shape[0] // 2
    groups = lead_groups(chunks)
    side = scalars[0]
    for place, ref in enumerate((first, second)):
        held[...] = jnp.swapaxes(ref[...], 0, 1)
        for chunk in range(chunks):
            outs[chunk][place] = held[(1 - side) * chunks + chunk]
            kept = outs[chunks + group_of(groups, chunk)]
            kept[place_of(groups, chunk), place] = held[side * chunks + chunk]


def split_pair(scalars, first, second):
    tok, heads_here, head_dim = first.shape
    steps = TPS // 2
    block = tok // steps
    chunks = heads_here // 2
    sizes = [len(members) for members in lead_groups(chunks)]
    spec = pl.BlockSpec((block, heads_here, head_dim), lambda i: (i, 0, 0))
    out_spec = pl.BlockSpec((2, block, head_dim), lambda i: (0, i, 0))
    outs = pl.pallas_call(
        split_kernel,
        grid=(steps,),
        out_shape=(jax.ShapeDtypeStruct((2, tok, head_dim), first.dtype),) * chunks
        + tuple(jax.ShapeDtypeStruct((size, 2, tok, head_dim), first.dtype) for size in sizes),
        in_specs=[pl.BlockSpec(memory_space=pltpu.SMEM), spec, spec],
        out_specs=(out_spec,) * chunks
        + tuple(pl.BlockSpec((size, 2, block, head_dim), lambda i: (0, 0, i, 0)) for size in sizes),
        scratch_shapes=[pltpu.VMEM((heads_here, block, head_dim), first.dtype)],
        compiler_params=ALL_VMEM,
        name="split_pair",
    )(scalars, first, second)
    return outs[:chunks], outs[chunks:]


def spread_kernel(scalars, queries, out_grad, *refs):
    outs, held_q, held_do = refs[:-2], refs[-2], refs[-1]
    side = scalars[0]
    heads_here = held_q.shape[0]
    chunks = heads_here // 2
    row_count = held_do.shape[0] // heads_here
    leads = query_groups(chunks)
    held_q[...] = jnp.swapaxes(queries[...], 0, 1)
    outs[0][...] = held_q[pl.ds(side * chunks, chunks)]
    for index, members in enumerate(leads):
        outs[1 + index][...] = held_q[pl.ds((1 - side) * chunks + members[0], len(members))]
    held_do[...] = jnp.swapaxes(out_grad[...], 0, 1)
    for out, members in zip(outs[1 + len(leads) :], chunk_groups(chunks)):
        for group in range(2):
            for row in range(row_count):
                head = row * heads_here + group * chunks + members[0]
                out[group * row_count + row] = held_do[head : head + len(members)]


def spread(scalars, queries, out_grad):
    tok, heads_here, head_dim = queries.shape
    part, heads, _ = out_grad.shape
    steps = min(TPS // 2, part // 16)
    chunks = heads_here // 2
    targets = 2 * heads // heads_here
    q_sizes = [chunks] + [len(members) for members in query_groups(chunks)]
    do_sizes = [len(members) for members in chunk_groups(chunks)]
    outs = pl.pallas_call(
        spread_kernel,
        grid=(steps,),
        out_shape=tuple(
            jax.ShapeDtypeStruct((size, tok, head_dim), queries.dtype) for size in q_sizes
        )
        + tuple(
            jax.ShapeDtypeStruct((targets, size, part, head_dim), queries.dtype)
            for size in do_sizes
        ),
        in_specs=[
            pl.BlockSpec(memory_space=pltpu.SMEM),
            pl.BlockSpec((tok // steps, heads_here, head_dim), lambda i: (i, 0, 0)),
            pl.BlockSpec((part // steps, heads, head_dim), lambda i: (i, 0, 0)),
        ],
        out_specs=tuple(
            pl.BlockSpec((size, tok // steps, head_dim), lambda i: (0, i, 0)) for size in q_sizes
        )
        + tuple(
            pl.BlockSpec((targets, size, part // steps, head_dim), lambda i: (0, 0, i, 0))
            for size in do_sizes
        ),
        scratch_shapes=[
            pltpu.VMEM((heads_here, tok // steps, head_dim), queries.dtype),
            pltpu.VMEM((heads, part // steps, head_dim), queries.dtype),
        ],
        compiler_params=ALL_VMEM,
        name="spread",
    )(scalars, queries, out_grad)
    return outs[0], outs[1 : len(q_sizes)], outs[len(q_sizes) :]


def merge_kernel(scalars, own_keep, own_recv, add_keep, add_recv, *refs):
    query_grads, out = refs[:-1], refs[-1]
    targets, _, part, head_dim = out.shape
    row_count = targets // 2
    side = scalars[0]
    factors = (head_dim ** (-0.5), 1.0)
    sums = ((own_keep, add_keep, side), (own_recv, add_recv, 1 - side))
    for which, (own, add, place) in enumerate(sums):
        for row in range(row_count):
            rows = pl.ds(row * part, part)
            target = place * row_count + row
            for plane, factor in enumerate(factors):
                total = own[plane, rows, :] * factor + add[plane, rows, :].astype(jnp.float32)
                out[target, plane] = total.astype(out.dtype)
            for plane, grad in enumerate(query_grads[which::2]):
                out[target, 2 + plane] = grad[rows, :]


def merge(scalars, row_count, own_keep, own_recv, add_keep, add_recv, query_grads):
    _, tok, head_dim = own_keep.shape
    vmem = pl.BlockSpec(memory_space=pltpu.VMEM)
    flat = [grad for pair in query_grads for grad in pair]
    shape = (2 * row_count, 2 + len(query_grads), tok // row_count, head_dim)
    return pl.pallas_call(
        merge_kernel,
        out_shape=jax.ShapeDtypeStruct(shape, jnp.bfloat16),
        in_specs=[pl.BlockSpec(memory_space=pltpu.SMEM)] + [vmem] * (4 + len(flat)),
        out_specs=vmem,
        compiler_params=ALL_VMEM,
        name="merge",
    )(scalars, own_keep, own_recv, add_keep, add_recv, *flat)


def query_place(chunk):
    return (0, 2) if chunk == 0 else (chunk - 1, 3 if chunk == 1 else 2)


def assemble_kernel(sources, *refs):
    count = len(refs) - 1 - len(sources)
    pieces, outs, held = refs[:count], refs[count:-1], refs[-1]
    row_count = pieces[0].shape[0] // 2
    for source, out in zip(sources, outs):
        chunks = len(source)
        for chunk, (message, plane) in enumerate(source):
            for group in range(2):
                for row in range(row_count):
                    head = row * 2 * chunks + group * chunks + chunk
                    held[head] = pieces[message][group * row_count + row, plane]
        out[...] = jnp.swapaxes(held[...], 0, 1)


def assemble(pieces, sources):
    senders, _, part, head_dim = pieces[0].shape
    heads = len(sources[0]) * senders
    steps = min(TPS // 2, part // 16)
    block = part // steps
    return pl.pallas_call(
        functools.partial(assemble_kernel, sources),
        grid=(steps,),
        out_shape=(jax.ShapeDtypeStruct((part, heads, head_dim), jnp.bfloat16),) * len(sources),
        in_specs=[
            pl.BlockSpec((senders, piece.shape[1], block, head_dim), lambda i: (0, 0, i, 0))
            for piece in pieces
        ],
        out_specs=(pl.BlockSpec((block, heads, head_dim), lambda i: (i, 0, 0)),) * len(sources),
        scratch_shapes=[pltpu.VMEM((heads, block, head_dim), jnp.bfloat16)],
        compiler_params=ALL_VMEM,
        name="assemble",
    )(*pieces)


def on_device(mesh_shape, queries, keys, values, out_grad, col_start, valid_tiles):
    _, heads_here, _ = queries.shape
    row_count = mesh_shape["row"]
    slab_total = mesh_shape["slab"]
    chunks = heads_here // 2
    slab_pos = lax.axis_index("slab")
    parity = slab_pos % 2
    partner = slab_pos + 1 - 2 * parity

    swap = [(s, s ^ 1) for s in range(slab_total)]
    out_high = [(s, s - 2 if s % 2 == 0 else s + 2) for s in range(slab_total)]
    out_high = [(s, t) for s, t in out_high if 0 <= t < slab_total]
    out_low = [(s, s + 2 if s % 2 == 0 else s - 2) for s in range(slab_total)]
    out_low = [(s, t) for s, t in out_low if 0 <= t < slab_total]

    def turned(pairs):
        return [(t, s) for s, t in pairs]

    def over_slab(array, pairs):
        return lax.ppermute(array, "slab", pairs)

    groups = [
        list(range(first, first + 2 * row_count))
        for first in range(0, slab_total * row_count, 2 * row_count)
    ]

    def to_all(array):
        return lax.all_to_all(
            array, ("slab", "row"), 0, 0, axis_index_groups=groups, tiled=True
        )

    slab_ids = jnp.stack(
        [
            jnp.where(parity == 0, slab_pos - 1, slab_pos + 1),
            slab_pos,
            partner,
            jnp.where(parity == 0, slab_pos + 2, slab_pos - 2),
        ]
    )
    inside = (slab_ids >= 0) & (slab_ids < slab_total)
    counts = jnp.where(inside, valid_tiles[jnp.clip(slab_ids, 0, slab_total - 1)], 0)
    places = parity.reshape(1)
    scalars = jnp.concatenate(
        [
            lax.dynamic_slice_in_dim(col_start, slab_pos * TPS, TPS, 0),
            lax.dynamic_slice_in_dim(col_start, partner * TPS, TPS, 0),
            counts.astype(jnp.int32),
            places,
        ]
    )

    leads, do_groups = lead_groups(chunks), chunk_groups(chunks)
    kv_sent, kv_keep = split_pair(places, keys, values)
    q_keep, q_sent, do_sent = spread(places, queries, out_grad)
    do_recv = [to_all(sent) for sent in do_sent]
    kv_high = [over_slab(kept, out_high) for kept in kv_keep]
    q_recv = [over_slab(sent, swap) for sent in q_sent]
    inputs = []
    for chunk in range(chunks):
        kv_recv = over_slab(kv_sent[chunk], swap)
        kv_low = over_slab(kv_recv, out_low)
        lead, do_all = group_of(leads, chunk), do_recv[group_of(do_groups, chunk)]
        q_other = q_recv[group_of(query_groups(chunks), chunk)]
        inputs.append(
            (chunk, q_keep, q_other, do_all, kv_low, kv_keep[lead], kv_recv, kv_high[lead])
        )

    query_grads = []
    partial_sums = []
    for chunk in range(chunks):
        dq_keep, dq_recv, own_keep, own_recv, half_low, half_high = attention_call(
            scalars, *inputs[chunk]
        )
        add_keep = over_slab(half_high, turned(out_high))
        add_recv = over_slab(half_low, turned(out_low))
        query_grads.append((dq_keep, dq_recv))
        partial_sums.append((own_keep, own_recv, add_keep, add_recv))
    pieces = []
    for chunk in range(chunks):
        own = [query_grads[other] for other in range(chunks) if query_place(other)[0] == chunk]
        merged = merge(places, row_count, *partial_sums[chunk], own)
        pieces.append(to_all(merged))
    query_sources = [query_place(chunk) for chunk in range(chunks)]
    used = 1 + max(message for message, _ in query_sources)
    (query_grad,) = assemble(pieces[:used], [query_sources])
    key_grad, value_grad = assemble(
        pieces, [[(chunk, plane) for chunk in range(chunks)] for plane in range(2)]
    )
    return query_grad, key_grad, value_grad


def solution(mesh):
    placed = (
        P("slab", "row", None),
        P("slab", "row", None),
        P("slab", "row", None),
        P(("slab", "row"), None, None),
        P(),
        P(),
    )

    def body(*operands):
        return on_device(dict(mesh.shape), *operands)

    return jax.shard_map(
        body,
        mesh=mesh,
        in_specs=placed,
        out_specs=(P(("slab", "row"), None, None),) * 3,
        check_vma=False,
    )
```

```python
import functools
import math

import jax
import jax.numpy as jnp
from jax import lax
from jax.experimental import pallas as pl
from jax.experimental.pallas import tpu as pltpu
from jax.sharding import PartitionSpec as P


TILE = 128
GH = 2
GW = 4
WIN_COLS = 2
TPS = GH * GW
SPAN = WIN_COLS * TILE
NEG = -1e30

ALL_VMEM = pltpu.CompilerParams(vmem_limit_bytes=67_043_328)


def chunk_groups(chunks):
    first = max(1, chunks // 2)
    return [range(first)] + ([range(first, chunks)] if first < chunks else [])


def lead_groups(chunks):
    return [range(1)] + ([range(1, chunks)] if chunks > 1 else [])


def query_groups(chunks):
    bounds = [0, 1, 2, chunks]
    return [range(a, min(b, chunks)) for a, b in zip(bounds, bounds[1:]) if a < min(b, chunks)]


def group_of(groups, chunk):
    return next(index for index, members in enumerate(groups) if chunk in members)


def place_of(groups, chunk):
    return groups[group_of(groups, chunk)].index(chunk)


def attention_kernel(
    chunk,
    scalars,
    q_keep,
    q_recv,
    do_ref,
    kv_low,
    kv_keep,
    kv_recv,
    kv_high,
    dq_keep,
    dq_recv,
    own_keep,
    own_recv,
    half_low,
    half_high,
    q_buf,
    do_buf,
    k_buf,
    v_buf,
    low_buf,
    high_buf,
    own_buf,
    dk_acc,
    dv_acc,
    p_buf,
    dp_buf,
    sems,
):
    _, tok, head_dim = q_keep.shape
    chunks = q_keep.shape[0]
    scale = head_dim ** (-0.5)
    parity = scalars[2 * TPS + 4]
    senders, _, part, _ = do_ref.shape
    do_place = place_of(chunk_groups(chunks), chunk)
    place = place_of(lead_groups(chunks), chunk)
    kv_keep, kv_high = kv_keep.at[place], kv_high.at[place]
    q_recv = q_recv.at[place_of(query_groups(chunks), chunk)]
    q_keep = q_keep.at[chunk]
    count = 0

    def begin(source, target):
        nonlocal count
        copy = pltpu.make_async_copy(source, target, sems.at[count])
        count += 1
        copy.start()
        return copy

    loads = []
    for slot, ref in enumerate((kv_low, kv_keep, kv_recv, kv_high)):
        rows = pl.ds(slot * tok, tok)
        if slot == 1:
            loads += [begin(q_keep, q_buf.at[pl.ds(0, tok), :])]
            for sender in range(senders):
                rows_do = pl.ds(sender * part, part)
                loads += [begin(do_ref.at[sender, do_place], do_buf.at[rows_do, :])]
        late = [begin(ref.at[0], k_buf.at[rows, :]), begin(ref.at[1], v_buf.at[rows, :])]
        loads += late if slot < 3 else []
    late += [begin(q_recv, q_buf.at[pl.ds(tok, tok), :])]
    dk_acc[...] = jnp.zeros_like(dk_acc)
    dv_acc[...] = jnp.zeros_like(dv_acc)
    for copy in loads:
        copy.wait()

    def unit(side, col, q_starts):
        width = TILE * len(q_starts)
        turn = ((side + parity) % 2 - side) * tok

        def rows_of(buf, shift):
            parts = [
                buf[pl.ds(pl.multiple_of(start + shift, TILE), TILE), :] for start in q_starts
            ]
            return parts[0] if len(parts) == 1 else jnp.concatenate(parts, axis=0)

        q = rows_of(q_buf, 0)
        do = rows_of(do_buf, turn)
        blocks = 3 * GH
        offsets = []
        limits = []
        for block in range(blocks):
            step, grid_row = block // GH, block % GH
            offset = (side + step) * tok + grid_row * GW * TILE + col * TILE
            offsets.append(pl.multiple_of(offset, TILE))
            count = scalars[2 * TPS + side + step]
            limits.append((count - grid_row * GW - col) * TILE)
        key_row = lax.broadcasted_iota(jnp.int32, (SPAN, width), 0)
        top = jnp.full((8, width), NEG, jnp.float32)
        for block in range(blocks):
            scores = lax.dot_general(
                k_buf[pl.ds(offsets[block], SPAN), :],
                q,
                (((1,), (1,)), ((), ())),
                preferred_element_type=jnp.float32,
            )
            if block != GH:
                scores = jnp.where(key_row < limits[block], scores, NEG)
            p_buf[pl.ds(block * SPAN, SPAN), pl.ds(0, width)] = scores
            top = jnp.maximum(top, jnp.max(scores.reshape(SPAN // 8, 8, width), axis=0))
        top = jnp.max(top, axis=0, keepdims=True)
        total = jnp.zeros((8, width), jnp.float32)
        delta = jnp.zeros((8, width), jnp.float32)
        for block in range(blocks):
            here = pl.ds(block * SPAN, SPAN), pl.ds(0, width)
            expo = jnp.exp2((p_buf[here] - top) * (scale * math.log2(math.e)))
            grad = lax.dot_general(
                v_buf[pl.ds(offsets[block], SPAN), :],
                do,
                (((1,), (1,)), ((), ())),
                preferred_element_type=jnp.float32,
            )
            p_buf[here] = expo
            dp_buf[here] = grad
            total += jnp.sum(expo.reshape(SPAN // 8, 8, width), axis=0)
            delta += jnp.sum((expo * grad).reshape(SPAN // 8, 8, width), axis=0)
        inverse = 1.0 / jnp.sum(total, axis=0, keepdims=True)
        delta = jnp.sum(delta, axis=0, keepdims=True) * inverse
        dq = jnp.zeros((width, head_dim), jnp.float32)
        for block in range(blocks):
            here = pl.ds(block * SPAN, SPAN), pl.ds(0, width)
            keys_here = pl.ds(offsets[block], SPAN)
            attend = p_buf[here] * inverse
            grad_scores = (attend * (dp_buf[here] - delta)).astype(jnp.bfloat16)
            attend_b = attend.astype(jnp.bfloat16)
            dv_acc[keys_here, :] += jnp.dot(attend_b, do, preferred_element_type=jnp.float32)
            dk_acc[keys_here, :] += jnp.dot(grad_scores, q, preferred_element_type=jnp.float32)
            dq += lax.dot_general(
                grad_scores,
                k_buf[keys_here, :],
                (((0,), (0,)), ((), ())),
                preferred_element_type=jnp.float32,
            )
        dq = (dq * scale).astype(jnp.bfloat16)
        for place, start in enumerate(q_starts):
            q_buf[pl.ds(start, TILE), :] = dq[place * TILE : (place + 1) * TILE]

    def run_side(side):
        def tile_at(index):
            column, which = index // GH, index % GH
            first = scalars[side * TPS + column]
            second = scalars[side * TPS + GW + column]
            row = jnp.where(first <= second, which, GH - 1 - which)
            start = side * tok + (row * GW + column) * TILE
            return jnp.where(row == 0, first, second), pl.multiple_of(start, TILE)

        def step(index):
            col, start = tile_at(index)
            next_col, next_start = tile_at(jnp.minimum(index + 1, TPS - 1))
            double = (index + 1 < TPS) & (col == next_col)

            @pl.when(double)
            def _():
                unit(side, col, [start, next_start])

            @pl.when(jnp.logical_not(double))
            def _():
                unit(side, col, [start])

            return index + 1 + double.astype(jnp.int32)

        lax.while_loop(lambda index: index < TPS, step, jnp.int32(0))

    run_side(0)
    for copy in late:
        copy.wait()
    stores = [begin(q_buf.at[pl.ds(0, tok), :], dq_keep)]
    low_buf[0] = (dk_acc[pl.ds(0, tok), :] * scale).astype(low_buf.dtype)
    low_buf[1] = dv_acc[pl.ds(0, tok), :].astype(low_buf.dtype)
    stores += [begin(low_buf, half_low)]
    run_side(1)
    stores += [begin(q_buf.at[pl.ds(tok, tok), :], dq_recv)]
    for slot, ref in ((1, own_keep), (2, own_recv)):
        rows = pl.ds(slot * tok, tok)
        own_buf[slot - 1, 0] = (dk_acc[rows, :] * scale).astype(own_buf.dtype)
        own_buf[slot - 1, 1] = dv_acc[rows, :].astype(own_buf.dtype)
        stores += [begin(own_buf.at[slot - 1], ref)]
    high_buf[0] = (dk_acc[pl.ds(3 * tok, tok), :] * scale).astype(high_buf.dtype)
    high_buf[1] = dv_acc[pl.ds(3 * tok, tok), :].astype(high_buf.dtype)
    stores += [begin(high_buf, half_high)]
    for copy in stores:
        copy.wait()


def attention_call(scalars, chunk, q_keep, q_recv, do_all, kv_low, kv_keep, kv_recv, kv_high):
    _, tok, head_dim = q_keep.shape
    senders = do_all.shape[0]
    place = pl.BlockSpec(memory_space=pl.ANY)
    keys_all = 4 * tok
    window = 3 * GH * SPAN
    pairs = 2 * TPS * TILE * window
    return pl.pallas_call(
        functools.partial(attention_kernel, chunk),
        out_shape=(jax.ShapeDtypeStruct((tok, head_dim), jnp.bfloat16),) * 2
        + (jax.ShapeDtypeStruct((2, tok, head_dim), jnp.bfloat16),) * 4,
        in_specs=[pl.BlockSpec(memory_space=pltpu.SMEM)] + [place] * 7,
        out_specs=(place,) * 6,
        scratch_shapes=[
            pltpu.VMEM((2 * tok, head_dim), jnp.bfloat16),
            pltpu.VMEM((2 * tok, head_dim), jnp.bfloat16),
            pltpu.VMEM((keys_all, head_dim), jnp.bfloat16),
            pltpu.VMEM((keys_all, head_dim), jnp.bfloat16),
            pltpu.VMEM((2, tok, head_dim), jnp.bfloat16),
            pltpu.VMEM((2, tok, head_dim), jnp.bfloat16),
            pltpu.VMEM((2, 2, tok, head_dim), jnp.bfloat16),
            pltpu.VMEM((keys_all, head_dim), jnp.float32),
            pltpu.VMEM((keys_all, head_dim), jnp.float32),
            pltpu.VMEM((window, GH * TILE), jnp.float32),
            pltpu.VMEM((window, GH * TILE), jnp.float32),
            pltpu.SemaphoreType.DMA((16 + senders,)),
        ],
        cost_estimate=pl.CostEstimate(
            flops=10 * pairs * head_dim, transcendentals=pairs, bytes_accessed=16 * tok * head_dim * 2
        ),
        compiler_params=ALL_VMEM,
        name="window_grads",
    )(scalars, q_keep, q_recv, do_all, kv_low, kv_keep, kv_recv, kv_high)


def split_kernel(scalars, *refs):
    (first, second), outs, held = refs[:2], refs[2:-1], refs[-1]
    chunks = held.shape[0] // 2
    groups = lead_groups(chunks)
    side = scalars[0]
    for place, ref in enumerate((first, second)):
        held[...] = jnp.swapaxes(ref[...], 0, 1)
        for chunk in range(chunks):
            outs[chunk][place] = held[(1 - side) * chunks + chunk]
            kept = outs[chunks + group_of(groups, chunk)]
            kept[place_of(groups, chunk), place] = held[side * chunks + chunk]


def split_pair(scalars, first, second):
    tok, heads_here, head_dim = first.shape
    steps = TPS // 2
    block = tok // steps
    chunks = heads_here // 2
    sizes = [len(members) for members in lead_groups(chunks)]
    spec = pl.BlockSpec((block, heads_here, head_dim), lambda i: (i, 0, 0))
    out_spec = pl.BlockSpec((2, block, head_dim), lambda i: (0, i, 0))
    outs = pl.pallas_call(
        split_kernel,
        grid=(steps,),
        out_shape=(jax.ShapeDtypeStruct((2, tok, head_dim), first.dtype),) * chunks
        + tuple(jax.ShapeDtypeStruct((size, 2, tok, head_dim), first.dtype) for size in sizes),
        in_specs=[pl.BlockSpec(memory_space=pltpu.SMEM), spec, spec],
        out_specs=(out_spec,) * chunks
        + tuple(pl.BlockSpec((size, 2, block, head_dim), lambda i: (0, 0, i, 0)) for size in sizes),
        scratch_shapes=[pltpu.VMEM((heads_here, block, head_dim), first.dtype)],
        compiler_params=ALL_VMEM,
        name="split_pair",
    )(scalars, first, second)
    return outs[:chunks], outs[chunks:]


def spread_kernel(scalars, queries, out_grad, *refs):
    outs, held_q, held_do = refs[:-2], refs[-2], refs[-1]
    side = scalars[0]
    heads_here = held_q.shape[0]
    chunks = heads_here // 2
    row_count = held_do.shape[0] // heads_here
    leads = query_groups(chunks)
    held_q[...] = jnp.swapaxes(queries[...], 0, 1)
    outs[0][...] = held_q[pl.ds(side * chunks, chunks)]
    for index, members in enumerate(leads):
        outs[1 + index][...] = held_q[pl.ds((1 - side) * chunks + members[0], len(members))]
    held_do[...] = jnp.swapaxes(out_grad[...], 0, 1)
    for out, members in zip(outs[1 + len(leads) :], chunk_groups(chunks)):
        for group in range(2):
            for row in range(row_count):
                head = row * heads_here + group * chunks + members[0]
                out[group * row_count + row] = held_do[head : head + len(members)]


def spread(scalars, queries, out_grad):
    tok, heads_here, head_dim = queries.shape
    part, heads, _ = out_grad.shape
    steps = min(TPS // 2, part // 16)
    chunks = heads_here // 2
    targets = 2 * heads // heads_here
    q_sizes = [chunks] + [len(members) for members in query_groups(chunks)]
    do_sizes = [len(members) for members in chunk_groups(chunks)]
    outs = pl.pallas_call(
        spread_kernel,
        grid=(steps,),
        out_shape=tuple(
            jax.ShapeDtypeStruct((size, tok, head_dim), queries.dtype) for size in q_sizes
        )
        + tuple(
            jax.ShapeDtypeStruct((targets, size, part, head_dim), queries.dtype)
            for size in do_sizes
        ),
        in_specs=[
            pl.BlockSpec(memory_space=pltpu.SMEM),
            pl.BlockSpec((tok // steps, heads_here, head_dim), lambda i: (i, 0, 0)),
            pl.BlockSpec((part // steps, heads, head_dim), lambda i: (i, 0, 0)),
        ],
        out_specs=tuple(
            pl.BlockSpec((size, tok // steps, head_dim), lambda i: (0, i, 0)) for size in q_sizes
        )
        + tuple(
            pl.BlockSpec((targets, size, part // steps, head_dim), lambda i: (0, 0, i, 0))
            for size in do_sizes
        ),
        scratch_shapes=[
            pltpu.VMEM((heads_here, tok // steps, head_dim), queries.dtype),
            pltpu.VMEM((heads, part // steps, head_dim), queries.dtype),
        ],
        compiler_params=ALL_VMEM,
        name="spread",
    )(scalars, queries, out_grad)
    return outs[0], outs[1 : len(q_sizes)], outs[len(q_sizes) :]


def merge_kernel(scalars, own_keep, own_recv, add_keep, add_recv, *refs):
    query_grads, out = refs[:-1], refs[-1]
    targets, _, part, _ = out.shape
    row_count = targets // 2
    side = scalars[0]
    sums = ((own_keep, add_keep, side), (own_recv, add_recv, 1 - side))
    for which, (own, add, place) in enumerate(sums):
        for row in range(row_count):
            rows = pl.ds(row * part, part)
            target = place * row_count + row
            for plane in range(2):
                total = own[plane, rows, :].astype(jnp.float32)
                total += add[plane, rows, :].astype(jnp.float32)
                out[target, plane] = total.astype(out.dtype)
            for plane, grad in enumerate(query_grads[which::2]):
                out[target, 2 + plane] = grad[rows, :]


def merge(scalars, row_count, own_keep, own_recv, add_keep, add_recv, query_grads):
    _, tok, head_dim = own_keep.shape
    vmem = pl.BlockSpec(memory_space=pltpu.VMEM)
    flat = [grad for pair in query_grads for grad in pair]
    shape = (2 * row_count, 2 + len(query_grads), tok // row_count, head_dim)
    return pl.pallas_call(
        merge_kernel,
        out_shape=jax.ShapeDtypeStruct(shape, jnp.bfloat16),
        in_specs=[pl.BlockSpec(memory_space=pltpu.SMEM)] + [vmem] * (4 + len(flat)),
        out_specs=vmem,
        compiler_params=ALL_VMEM,
        name="merge",
    )(scalars, own_keep, own_recv, add_keep, add_recv, *flat)


def query_place(chunk):
    return (0, 2) if chunk == 0 else (chunk - 1, 3 if chunk == 1 else 2)


def assemble_kernel(sources, *refs):
    count = len(refs) - 1 - len(sources)
    pieces, outs, held = refs[:count], refs[count:-1], refs[-1]
    row_count = pieces[0].shape[0] // 2
    for source, out in zip(sources, outs):
        chunks = len(source)
        for chunk, (message, plane) in enumerate(source):
            for group in range(2):
                for row in range(row_count):
                    head = row * 2 * chunks + group * chunks + chunk
                    held[head] = pieces[message][group * row_count + row, plane]
        out[...] = jnp.swapaxes(held[...], 0, 1)


def assemble(pieces, sources):
    senders, _, part, head_dim = pieces[0].shape
    heads = len(sources[0]) * senders
    steps = min(TPS // 2, part // 16)
    block = part // steps
    return pl.pallas_call(
        functools.partial(assemble_kernel, sources),
        grid=(steps,),
        out_shape=(jax.ShapeDtypeStruct((part, heads, head_dim), jnp.bfloat16),) * len(sources),
        in_specs=[
            pl.BlockSpec((senders, piece.shape[1], block, head_dim), lambda i: (0, 0, i, 0))
            for piece in pieces
        ],
        out_specs=(pl.BlockSpec((block, heads, head_dim), lambda i: (i, 0, 0)),) * len(sources),
        scratch_shapes=[pltpu.VMEM((heads, block, head_dim), jnp.bfloat16)],
        compiler_params=ALL_VMEM,
        name="assemble",
    )(*pieces)


def on_device(mesh_shape, queries, keys, values, out_grad, col_start, valid_tiles):
    _, heads_here, _ = queries.shape
    row_count = mesh_shape["row"]
    slab_total = mesh_shape["slab"]
    chunks = heads_here // 2
    slab_pos = lax.axis_index("slab")
    parity = slab_pos % 2
    partner = slab_pos + 1 - 2 * parity

    swap = [(s, s ^ 1) for s in range(slab_total)]
    out_high = [(s, s - 2 if s % 2 == 0 else s + 2) for s in range(slab_total)]
    out_high = [(s, t) for s, t in out_high if 0 <= t < slab_total]
    out_low = [(s, s + 2 if s % 2 == 0 else s - 2) for s in range(slab_total)]
    out_low = [(s, t) for s, t in out_low if 0 <= t < slab_total]

    def turned(pairs):
        return [(t, s) for s, t in pairs]

    def over_slab(array, pairs):
        return lax.ppermute(array, "slab", pairs)

    groups = [
        list(range(first, first + 2 * row_count))
        for first in range(0, slab_total * row_count, 2 * row_count)
    ]

    def to_all(array):
        return lax.all_to_all(
            array, ("slab", "row"), 0, 0, axis_index_groups=groups, tiled=True
        )

    slab_ids = jnp.stack(
        [
            jnp.where(parity == 0, slab_pos - 1, slab_pos + 1),
            slab_pos,
            partner,
            jnp.where(parity == 0, slab_pos + 2, slab_pos - 2),
        ]
    )
    inside = (slab_ids >= 0) & (slab_ids < slab_total)
    counts = jnp.where(inside, valid_tiles[jnp.clip(slab_ids, 0, slab_total - 1)], 0)
    places = parity.reshape(1)
    scalars = jnp.concatenate(
        [
            lax.dynamic_slice_in_dim(col_start, slab_pos * TPS, TPS, 0),
            lax.dynamic_slice_in_dim(col_start, partner * TPS, TPS, 0),
            counts.astype(jnp.int32),
            places,
        ]
    )

    leads, do_groups = lead_groups(chunks), chunk_groups(chunks)
    kv_sent, kv_keep = split_pair(places, keys, values)
    q_keep, q_sent, do_sent = spread(places, queries, out_grad)
    do_recv = [to_all(sent) for sent in do_sent]
    kv_high = [over_slab(kept, out_high) for kept in kv_keep]
    q_recv = [over_slab(sent, swap) for sent in q_sent]
    inputs = []
    for chunk in range(chunks):
        kv_recv = over_slab(kv_sent[chunk], swap)
        kv_low = over_slab(kv_recv, out_low)
        lead, do_all = group_of(leads, chunk), do_recv[group_of(do_groups, chunk)]
        q_other = q_recv[group_of(query_groups(chunks), chunk)]
        inputs.append(
            (chunk, q_keep, q_other, do_all, kv_low, kv_keep[lead], kv_recv, kv_high[lead])
        )

    query_grads = []
    partial_sums = []
    for chunk in range(chunks):
        dq_keep, dq_recv, own_keep, own_recv, half_low, half_high = attention_call(
            scalars, *inputs[chunk]
        )
        add_keep = over_slab(half_high, turned(out_high))
        add_recv = over_slab(half_low, turned(out_low))
        query_grads.append((dq_keep, dq_recv))
        partial_sums.append((own_keep, own_recv, add_keep, add_recv))
    pieces = []
    for chunk in range(chunks):
        own = [query_grads[other] for other in range(chunks) if query_place(other)[0] == chunk]
        merged = merge(places, row_count, *partial_sums[chunk], own)
        pieces.append(to_all(merged))
    query_sources = [query_place(chunk) for chunk in range(chunks)]
    used = 1 + max(message for message, _ in query_sources)
    (query_grad,) = assemble(pieces[:used], [query_sources])
    key_grad, value_grad = assemble(
        pieces, [[(chunk, plane) for chunk in range(chunks)] for plane in range(2)]
    )
    return query_grad, key_grad, value_grad


def solution(mesh):
    placed = (
        P("slab", "row", None),
        P("slab", "row", None),
        P("slab", "row", None),
        P(("slab", "row"), None, None),
        P(),
        P(),
    )

    def body(*operands):
        return on_device(dict(mesh.shape), *operands)

    return jax.shard_map(
        body,
        mesh=mesh,
        in_specs=placed,
        out_specs=(P(("slab", "row"), None, None),) * 3,
        check_vma=False,
    )
```
